32 devices in a mesh: patch: 8 (over z, x), lev: 4 (over y, core).
Axes of the slice: x: 2, y: 2, z: 4, core: 2. Of those that a mesh axis runs over, the one named last changes fastest.
Arguments:
- increment_rhs: float32 [20, 65536], P('lev', 'patch'), may hold values from -6 to 6
- error_variance: float32 [20, 65536], P('lev', 'patch'), may hold values from 1 to 8
- perturbations: bfloat16 [40, 20, 65536], P(None, 'lev', 'patch'), may hold values from -6 to 6
- interp_slot: int32 [65536], P('patch'), may hold values from 0 to 510, as said below
- interp_weight: float32 [65536], P('patch'), may hold values from 0 to 1
- halo_rows: int32 [8], replicated, may hold values from 8 to 128, as said below
- vertical_coupling: float32 [20], replicated, may hold values from 0.1 to 0.45
Outputs:
- solution: float32 [20, 65536], P('lev', 'patch')
- residual: float32 [20, 65536], P('lev', 'patch')
The draws below stay inside these ranges and needn't reach their ends.
Inputs may be any that keep to these rules, and one draw needn't show every extreme that they name: `halo_rows`: each patch's count is 128 divided by 1, 2, 4, 8 or 16, and some patch has 128. `interp_slot`: the column with index c within its patch has slot c // 16 - 1 or c // 16, kept within 0 to 510.
All inputs are finite; a program needn't handle non-finite values.
Results may differ from the reference program's by a relative error of at most 0.0003.
Values sent between devices are 32-bit elements; how exact they have to be, the bound alone decides.
No kernel may reach another device: no remote copies, remote signals or barrier semaphores. Data moves between devices by JAX's collectives and lax.ppermute only.
A program may use at most 128 MiB of HBM per device.

```python
import math
import jax
import jax.numpy as jnp
from jax import lax

MEMBERS = 40
G_DEV = 8192
RATIO = 16
HALO = 128
ITERS = 4
SUB = 512
NPATCH = 8
COLUMNS = 65536
LEVELS = 20


def draw_halo_rows(key, part):
    exponents = jax.random.randint(jax.random.fold_in(key, 11), (NPATCH,), 0, 5)
    counts = jnp.right_shift(jnp.full((NPATCH,), HALO, jnp.int32), exponents.astype(jnp.int32))
    widest = jax.random.randint(jax.random.fold_in(key, 12), (), 0, NPATCH)
    return counts.at[widest].set(HALO).astype(jnp.int32)


def draw_interp_slot(key, part):
    columns = jnp.arange(COLUMNS, dtype=jnp.int32)
    base_point = columns % G_DEV // RATIO
    jitter = jax.random.randint(jax.random.fold_in(key, 21), (COLUMNS,), 0, 2).astype(jnp.int32)
    return jnp.clip(base_point - jitter, 0, SUB - 2).astype(jnp.int32)


def levels(rng, dims, split, smallest, high):
    factor_of = 1.0
    for axis_at, shards_of in split:
        draws = jax.random.uniform(jax.random.fold_in(jax.random.fold_in(rng, 6), axis_at), (shards_of,), jnp.float32, smallest / len(split), high / len(split))
        factor_of = factor_of * jnp.repeat(jnp.exp(draws), dims[axis_at] // shards_of).reshape((-1,) + (1,) * (len(dims) - 1 - axis_at))
    return factor_of


def gaussian(stream_key, shape, scale, most, cuts=(), kind=jnp.bfloat16):
    values = jax.random.normal(stream_key, shape, jnp.float32) * scale
    if len(cuts) > 0:
        values = levels(stream_key, shape, cuts, -0.22, 0.18) * values
    return jnp.clip(values, min=-most, max=most).astype(kind)


def setup_inputs(seed: int = 0) -> dict:
    seeds = jax.random.split(jax.random.key(seed), 8)
    increment_rhs = gaussian(seeds[0], (LEVELS, COLUMNS), 1.0, 6.0, ((0, 4), (1, 8)), jnp.float32)
    error_variance = jnp.clip(jnp.exp(math.log(8.0) - 2.0794415 * jax.random.uniform(seeds[1], (LEVELS, COLUMNS), jnp.float32) ** levels(seeds[1], (LEVELS, COLUMNS), ((0, 4), (1, 8)), -0.2, 0.2)), 1.0, 8.0)
    perturbations = gaussian(seeds[2], (MEMBERS, LEVELS, COLUMNS), 1.0, 6.0, ((1, 4), (2, 8)))
    interp_slot = draw_interp_slot(jax.random.fold_in(seeds[7], 71), 0)
    interp_weight = jnp.clip(1.0 * jax.random.uniform(seeds[4], (COLUMNS,), jnp.float32) ** levels(seeds[4], (COLUMNS,), ((0, 8),), -0.2, 0.2), 0.0, 1.0)
    halo_rows = draw_halo_rows(jax.random.fold_in(seeds[7], 71), 0)
    vertical_coupling = jnp.clip(jnp.exp(jax.random.uniform(seeds[6], (LEVELS,), jnp.float32, math.log(0.1), math.log(0.45))), 0.1, 0.45)
    return dict(increment_rhs=increment_rhs, error_variance=error_variance, perturbations=perturbations, interp_slot=interp_slot, interp_weight=interp_weight, halo_rows=halo_rows, vertical_coupling=vertical_coupling)


def tap_values(offsets):
    distance = jnp.minimum(jnp.abs(offsets), HALO + 1).astype(jnp.int32)
    residue = (97 * distance * distance + 31 * distance) % 257
    rough = 0.5 + residue.astype(jnp.float32) / 256.0
    taper = 1.0 - distance.astype(jnp.float32) / (2.0 * HALO)
    raw = jnp.where(distance <= HALO, taper * rough, 0.0)
    support = jnp.arange(0, HALO + 1).astype(jnp.int32)
    support_rough = 0.5 + ((97 * support * support + 31 * support) % 257).astype(jnp.float32) / 256.0
    support_taper = 1.0 - support.astype(jnp.float32) / (2.0 * HALO)
    support_squares = (support_taper * support_rough) ** 2
    normal = jnp.sqrt(2.0 * jnp.sum(support_squares) - support_squares[0])
    return raw / normal

def cycle_convolve(field):
    length = field.shape[1]
    places = jnp.arange(length)
    signed = jnp.where(places > length // 2, places - length, places).astype(jnp.float32)
    kernel = tap_values(signed)
    spectrum = jnp.fft.rfft(field, axis=1) * jnp.fft.rfft(kernel)[None, :]
    return jnp.fft.irfft(spectrum, n=length, axis=1)

def rim_blocks():
    rows = jnp.arange(HALO).astype(jnp.float32)[:, None]
    cols = jnp.arange(HALO).astype(jnp.float32)[None, :]
    return (tap_values(rows - cols - HALO), tap_values(HALO + rows - cols))

def horizontal(field, halo_rows, adjoint):
    first, third = rim_blocks()
    convolved = cycle_convolve(field).reshape(LEVELS, NPATCH, SUB)
    shaped = field.reshape(LEVELS, NPATCH, SUB)
    left_source = jnp.roll(shaped, 1, axis=1)[:, :, SUB - HALO:]
    right_source = jnp.roll(shaped, -1, axis=1)[:, :, :HALO]
    offsets = jnp.arange(HALO)
    if adjoint:
        left_count = jnp.roll(halo_rows, 1)
        right_count = jnp.roll(halo_rows, -1)
        drop_left = (offsets[None, :] >= left_count[:, None]).astype(jnp.float32)
        drop_right = ((HALO - 1 - offsets)[None, :] >= right_count[:, None]).astype(jnp.float32)
        from_left = jnp.einsum('lpa,ab->lpb', left_source, first, precision=lax.Precision.HIGHEST) * drop_left[None]
        from_right = jnp.einsum('lpa,ab->lpb', right_source, third, precision=lax.Precision.HIGHEST) * drop_right[None]
    else:
        drop_left = ((HALO - 1 - offsets)[None, :] >= halo_rows[:, None]).astype(jnp.float32)
        drop_right = (offsets[None, :] >= halo_rows[:, None]).astype(jnp.float32)
        from_left = jnp.einsum('lpa,ab->lpb', left_source * drop_left[None], first, precision=lax.Precision.HIGHEST)
        from_right = jnp.einsum('lpa,ab->lpb', right_source * drop_right[None], third, precision=lax.Precision.HIGHEST)
    convolved = convolved.at[:, :, :HALO].add(-from_left)
    convolved = convolved.at[:, :, SUB - HALO:].add(-from_right)
    return convolved.reshape(LEVELS, NPATCH * SUB)

def vertical_forward(field, coupling):
    padded = jnp.pad(field, ((1, 1), (0, 0)))
    return field + coupling[:, None] * (padded[:-2] + padded[2:])

def vertical_adjoint(field, coupling):
    padded = jnp.pad(coupling[:, None] * field, ((1, 1), (0, 0)))
    return field + padded[:-2] + padded[2:]

def reference(increment_rhs, error_variance, perturbations, interp_slot, interp_weight, halo_rows, vertical_coupling):
    patch_base = (jnp.arange(NPATCH) * SUB).astype(jnp.int32)[:, None]
    global_slot = (patch_base + interp_slot.reshape(NPATCH, G_DEV)).reshape(-1).astype(jnp.int32)
    weights = interp_weight[None, :]

    def covariance(direction):

        def one_member(total, member):
            pert = member.astype(jnp.float32)
            weighted = pert * direction
            subgrid = jnp.zeros((LEVELS, NPATCH * SUB), jnp.float32)
            subgrid = subgrid.at[:, global_slot].add(weighted * weights)
            subgrid = subgrid.at[:, global_slot + 1].add(weighted * (1.0 - weights))
            subgrid = horizontal(subgrid, halo_rows, False)
            subgrid = vertical_forward(subgrid, vertical_coupling)
            subgrid = vertical_adjoint(subgrid, vertical_coupling)
            subgrid = horizontal(subgrid, halo_rows, True)
            back = subgrid[:, global_slot] * weights + subgrid[:, global_slot + 1] * (1.0 - weights)
            return (total + pert * back, None)
        total, _ = lax.scan(one_member, jnp.zeros((LEVELS, COLUMNS), jnp.float32), perturbations)
        return error_variance * direction + total / (MEMBERS - 1)
    solution = jnp.zeros_like(increment_rhs)
    residual = increment_rhs
    direction = increment_rhs
    norm_now = jnp.sum(residual * residual)
    for iteration in range(ITERS):
        image = covariance(direction)
        alpha = norm_now / jnp.sum(direction * image)
        solution = solution + alpha * direction
        residual = residual - alpha * image
        norm_next = jnp.sum(residual * residual)
        direction = residual + norm_next / norm_now * direction
        norm_now = norm_next
    return (solution, residual)
```

```python
import functools

import jax
import jax.numpy as jnp
import numpy as np
from jax import lax
from jax.experimental import pallas as pl
from jax.experimental.pallas import tpu as pltpu
from jax.sharding import PartitionSpec as P

MEMBERS = 40
RATIO = 16
HALO = 128
ITERS = 4
LANES = 128
REACH = 2 * HALO
VMEM_LIMIT = 40 * 1024 * 1024


def tap_blocks():
    reach = np.arange(HALO + 1)
    rough = 0.5 + ((97 * reach * reach + 31 * reach) % 257) / 256.0
    raw = (1.0 - reach / (2.0 * HALO)) * rough
    taps = raw / np.sqrt(2.0 * np.sum(raw**2) - raw[0] ** 2)
    rows, cols = np.arange(HALO)[:, None], np.arange(HALO)[None, :]
    blocks = []
    for shift in range(3):
        distance = np.abs(rows - cols + (1 - shift) * HALO)
        blocks.append(np.where(distance <= HALO, taps[np.minimum(distance, HALO)], 0.0))
    return blocks


def block_products():
    blocks = tap_blocks()
    return np.stack([np.stack([a.T @ b for b in blocks]) for a in blocks]).astype(np.float32)


def band_kernel(counts_ref, prod_ref, hi_ref, lo_ref):
    own_blocks = hi_ref.shape[1] // HALO
    edge = (0, own_blocks + 1)
    lane = lax.broadcasted_iota(jnp.int32, (HALO, HALO), 1)
    row = lax.broadcasted_iota(jnp.int32, (HALO, HALO), 0)
    crossing = {
        (0, 2): (counts_ref[0], False),
        (1, 1): (counts_ref[1], True),
        (own_blocks, own_blocks + 2): (counts_ref[1], False),
        (own_blocks + 1, own_blocks + 1): (counts_ref[2], True),
    }

    def keep(index, key):
        count, from_end = crossing[key]
        return (HALO - 1 - index if from_end else index) < count

    for source in range(own_blocks + 4):
        for target in range(2, own_blocks + 2):
            total = jnp.zeros((HALO, HALO), jnp.float32)
            for i in range(edge[0], edge[1] + 1):
                a, b = source - i, target - i
                if not (0 <= a < 3 and 0 <= b < 3):
                    continue
                term = prod_ref[a, b]
                if (i, source) in crossing:
                    term = jnp.where(keep(row, (i, source)), term, 0.0)
                if (i, target) in crossing:
                    term = jnp.where(keep(lane, (i, target)), term, 0.0)
                total = total + term
            hi = total.astype(jnp.bfloat16)
            at = (pl.ds(source * HALO, HALO), pl.ds((target - 2) * HALO, HALO))
            hi_ref[at] = hi
            lo_ref[at] = (total - hi.astype(jnp.float32)).astype(jnp.bfloat16)


def to_subgrid(pert_ref, field_ref, weight_ref, part_refs, level_ref, side_ref):
    levels, ratio, points = field_ref.shape
    members = pert_ref.shape[1] // ratio
    tiles = members // 8

    def one_level(level):
        for lane_tile in range(points // LANES):
            lanes = pl.ds(lane_tile * LANES, LANES)
            field = field_ref[level, :, lanes]
            for j in range(3):
                level_ref[j] = field * weight_ref[j, lane_tile]
            total = [[None] * tiles for _ in range(3)]
            for r in range(ratio):
                scale = [level_ref[j, pl.ds(r, 8, stride=0), :] for j in range(3)]
                for t in range(tiles):
                    pert = pert_ref[level, pl.ds(r * members + 8 * t, 8), lanes]
                    for j in range(3):
                        term = pert * scale[j]
                        total[j][t] = term if total[j][t] is None else total[j][t] + term
            for j in range(3):
                for t in range(tiles):
                    side_ref[j, pl.ds(8 * t, 8), lanes] = total[j][t]
        return (
            side_ref[1]
            + pltpu.roll(side_ref[0], points - 1, axis=1)
            + pltpu.roll(side_ref[2], 1, axis=1)
        )

    first = 0
    for ref in part_refs:
        count = ref.shape[0] // members

        def body(k, carry, ref=ref, first=first):
            rows = pl.ds(pl.multiple_of(k * members, 8), members)
            ref[rows, :] = one_level(first + k)
            return carry

        lax.fori_loop(0, count, body, 0)
        first += count


def from_subgrid(pert_ref, level, values, weight_ref, side_ref, sum_ref, out_ref):
    members, points = values.shape
    ratio = out_ref.shape[0]
    tiles = members // 8
    side_ref[0] = pltpu.roll(values, 1, axis=1)
    side_ref[1] = values
    side_ref[2] = pltpu.roll(values, points - 1, axis=1)
    for lane_tile in range(points // LANES):
        lanes = pl.ds(lane_tile * LANES, LANES)
        near = [[side_ref[j, pl.ds(8 * t, 8), lanes] for t in range(tiles)] for j in range(3)]
        for r in range(ratio):
            total = [None] * 3
            for t in range(tiles):
                pert = pert_ref[level, pl.ds(r * members + 8 * t, 8), lanes]
                for j in range(3):
                    term = pert * near[j][t]
                    total[j] = term if total[j] is None else total[j] + term
            mixed = None
            for j in range(3):
                term = total[j] * weight_ref[j, lane_tile, pl.ds(r, 8, stride=0), :]
                mixed = term if mixed is None else mixed + term
            sum_ref[pl.ds(8 * r, 8), :] = mixed
        result = sum_ref[pl.ds(0, ratio, stride=8), :]
        for k in range(1, 8):
            result = result + sum_ref[pl.ds(k, ratio, stride=8), :]
        out_ref[:, lanes] = result


def split(x):
    hi = x.astype(jnp.bfloat16)
    return hi, (x - hi.astype(jnp.float32)).astype(jnp.bfloat16)


def band_product(pieces, hi_ref, lo_ref, out_ref):
    halves = [split(ref[...]) for ref in pieces]
    for block in range(out_ref.shape[1] // REACH):
        cols = pl.ds(block * REACH, REACH)
        total = None
        for k in range(block, block + 3):
            hi, lo = halves[k]
            rows = pl.ds(k * REACH, REACH)
            for left, right_ref in ((hi, hi_ref), (lo, hi_ref), (hi, lo_ref)):
                term = jnp.dot(left, right_ref[rows, cols], preferred_element_type=jnp.float32)
                total = term if total is None else total + term
        out_ref[:, cols] = total


def sums(dots_ref):
    total = jnp.sum(dots_ref[...], axis=0)
    return total[0:1], total[1:2]


def step_sizes(stage, dots_ref, scalar_ref):
    gamma, delta = sums(dots_ref)
    if stage == 1:
        return gamma, gamma / delta, None
    beta = gamma / scalar_ref[0:1]
    alpha = gamma / (delta - beta * gamma / scalar_ref[1:2])
    return gamma, alpha, beta


STATE_IN = {0: "r", 1: "rw", 2: "zspxrw", 3: "zspxrw"}
STATE_OUT = {0: "w", 1: "zxrw", 2: "zspxrw", 3: "spxrw"}


def apply_kernel(stage, parts, *refs):
    refs = list(refs)
    take = lambda n: [refs.pop(0) for _ in range(n)]
    pieces = take(4)
    hi_ref, lo_ref, pert_ref, weight_ref, error_ref = take(5)
    dots_in, scalar_in = take(2) if stage else (None, None)
    state = dict(zip(STATE_IN[stage], take(len(STATE_IN[stage]))))
    new = dict(zip(STATE_OUT[stage], take(len(STATE_OUT[stage]))))
    (dots_out,) = take(1)
    (scalar_out,) = take(1) if stage else (None,)
    part_refs = take(parts)
    conv_ref, side_ref, level_ref, sum_ref, image_ref = refs

    levels, ratio, points = error_ref.shape
    members = pert_ref.shape[1] // ratio
    band_product(pieces, hi_ref, lo_ref, conv_ref)

    alpha = beta = None
    if stage:
        gamma, alpha, beta = step_sizes(stage, dots_in, scalar_in)
        scalar_out[0:1] = gamma
        scalar_out[1:2] = alpha
        alpha = jnp.concatenate([alpha] * (points // LANES), axis=1)
        if beta is not None:
            beta = jnp.concatenate([beta] * (points // LANES), axis=1)

    def one_level(level, carry):
        rows = pl.ds(pl.multiple_of(level * members, 8), members)
        from_subgrid(pert_ref, level, conv_ref[rows, :], weight_ref, side_ref, sum_ref, image_ref)
        mean = image_ref[...] * (1.0 / (MEMBERS - 1))
        r = state["r"][level]
        if stage == 0:
            w = error_ref[level] * r + mean
            new["w"][level] = w
        else:
            w = state["w"][level]
            z = error_ref[level] * w + mean
            s, p = w, r
            if stage > 1:
                z = z + beta * state["z"][level]
                s = s + beta * state["s"][level]
                p = p + beta * state["p"][level]
            x = alpha * p
            if stage > 1:
                x = x + state["x"][level]
            r = r - alpha * s
            w = w - alpha * z
            for name, value in dict(z=z, s=s, p=p, x=x, r=r, w=w).items():
                if name in new:
                    new[name][level] = value
        return carry[0] + r * r, carry[1] + r * w

    zero = jnp.zeros((ratio, points), jnp.float32)
    total = lax.fori_loop(0, levels, one_level, (zero, zero))
    partial = [jnp.broadcast_to(jnp.sum(t, keepdims=True), (1, LANES)) for t in total]
    partial = jnp.concatenate(partial, axis=0)
    dots_out[...] = jnp.broadcast_to(partial[None], dots_out.shape)
    if parts:
        to_subgrid(pert_ref, new["w"], weight_ref, part_refs, level_ref, side_ref)


def final_kernel(dots_ref, scalar_ref, s_ref, p_ref, x_ref, r_ref, w_ref, x_out, r_out):
    points = x_ref.shape[2]
    _, alpha, beta = step_sizes(ITERS - 1, dots_ref, scalar_ref)
    alpha = jnp.concatenate([alpha] * (points // LANES), axis=1)
    beta = jnp.concatenate([beta] * (points // LANES), axis=1)
    for level in range(x_ref.shape[0]):
        s = w_ref[level] + beta * s_ref[level]
        p = r_ref[level] + beta * p_ref[level]
        x_out[level] = x_ref[level] + alpha * p
        r_out[level] = r_ref[level] - alpha * s


def vertical_kernel(coupling_ref, below_ref, *refs):
    *own_refs, above_ref, left_ref, right_ref = refs
    where = []
    for ref in (below_ref, *own_refs, above_ref):
        for k in range(ref.shape[0] // MEMBERS):
            where.append((ref, k * MEMBERS))
    levels = len(where) - 4

    def body(t, carry):
        field = [ref[pl.ds(base + pl.multiple_of(t * 8, 8), 8), :] for ref, base in where]
        stepped = [
            field[l + 1] + coupling_ref[l] * (field[l] + field[l + 2]) for l in range(levels + 2)
        ]
        scaled = [coupling_ref[l] * stepped[l] for l in range(levels + 2)]
        for l in range(levels):
            value = stepped[l + 1] + (scaled[l] + scaled[l + 2])
            rows = pl.ds(l * MEMBERS + pl.multiple_of(t * 8, 8), 8)
            left_ref[rows, :] = value[:, :REACH]
            right_ref[rows, :] = value[:, value.shape[1] - REACH :]
        return carry

    lax.fori_loop(0, MEMBERS // 8, body, 0)


def start_kernel(parts, field_ref, pert_ref, weight_ref, *refs):
    part_refs, (level_ref, side_ref) = refs[:parts], refs[parts:]
    to_subgrid(pert_ref, field_ref, weight_ref, part_refs, level_ref, side_ref)


def whole():
    return pl.BlockSpec(memory_space=pltpu.VMEM)


def scalars():
    return pl.BlockSpec(memory_space=pltpu.SMEM)


def call(kernel, args, out_shape, scratch=(), flops=0, in_specs=None):
    size = sum(np.prod(a.shape) * a.dtype.itemsize for a in args)
    return pl.pallas_call(
        kernel,
        in_specs=in_specs or [whole()] * len(args),
        out_specs=jax.tree.map(lambda _: whole(), out_shape),
        out_shape=out_shape,
        scratch_shapes=list(scratch),
        compiler_params=pltpu.CompilerParams(vmem_limit_bytes=VMEM_LIMIT),
        cost_estimate=pl.CostEstimate(flops=flops, bytes_accessed=int(size), transcendentals=0),
    )(*args)


def f32(*shape):
    return jax.ShapeDtypeStruct(shape, jnp.float32)


def shift(block, axis, step, periodic):
    count = lax.axis_size(axis)
    pairs = [(i, (i + step) % count) for i in range(count) if periodic or 0 <= i + step < count]
    return lax.ppermute(block, axis, pairs)


def shards(
    increment_rhs,
    error_variance,
    perturbations,
    interp_slot,
    interp_weight,
    halo_rows,
    vertical_coupling,
):
    members, levels, columns = perturbations.shape
    points = columns // RATIO
    devices = lax.axis_size("patch") * lax.axis_size("lev")

    def fold(a):
        return jnp.swapaxes(a.reshape(a.shape[:-1] + (points, RATIO)), -1, -2)

    rhs, error = fold(increment_rhs), fold(error_variance)
    pert = perturbations.reshape(members, levels, points, RATIO).transpose(1, 3, 0, 2)
    pert = pert.astype(jnp.float32).reshape(levels, RATIO * members, points)

    is_lower = interp_slot < jnp.arange(columns) // RATIO
    weights = fold(
        jnp.stack(
            [
                jnp.where(is_lower, interp_weight, 0.0),
                jnp.where(is_lower, 1.0 - interp_weight, interp_weight),
                jnp.where(is_lower, 0.0, 1.0 - interp_weight),
            ]
        )
    )
    weights = jnp.swapaxes(weights.reshape(3, RATIO, points // LANES, LANES), 1, 2)

    patch, patches = lax.axis_index("patch"), lax.axis_size("patch")
    near = (patch + jnp.array([patches - 1, 0, 1])) % patches
    extended = points + 2 * REACH
    band_hi, band_lo = call(
        band_kernel,
        (halo_rows[near], jnp.asarray(block_products())),
        (jax.ShapeDtypeStruct((extended, points), jnp.bfloat16),) * 2,
        in_specs=[scalars(), whole()],
    )
    first_level = lax.axis_index("lev") * levels
    coupling = lax.dynamic_slice(jnp.pad(vertical_coupling, 1), (first_level,), (levels + 2,))

    part_levels = (2, levels - 4, 2)
    part_shapes = tuple(f32(n * members, points) for n in part_levels)
    level_scratch = pltpu.VMEM((3, RATIO, LANES), jnp.float32)
    side_scratch = pltpu.VMEM((3, members, points), jnp.float32)
    grid_shape = f32(levels, RATIO, points)

    def extend(parts, dots):
        low, middle, high = parts
        from_below = shift(high, "lev", 1, False)
        from_above = shift(low, "lev", -1, False)
        half = f32(levels * members, REACH)
        left, right = call(
            vertical_kernel,
            (coupling, from_below, low, middle, high, from_above),
            (half, half),
            in_specs=[scalars()] + [whole()] * 5,
        )
        if dots is not None:
            dots, left, right = lax.optimization_barrier((dots, left, right))
        from_left = shift(right, "patch", 1, True)
        from_right = shift(left, "patch", -1, True)
        if dots is not None:
            dots = lax.all_to_all(dots, ("patch", "lev"), 0, 0, tiled=True)
        return (from_left, left, right, from_right), dots

    def apply(stage, pieces, dots, scalar, state):
        outs = [grid_shape] * len(STATE_OUT[stage]) + [f32(devices, 2, LANES)]
        outs += [f32(8, LANES)] if stage else []
        last = stage == ITERS - 1
        outs += [] if last else list(part_shapes)
        args = [*pieces, band_hi, band_lo, pert, weights, error]
        args += [dots, scalar] if stage else []
        args += [state[name] for name in STATE_IN[stage]]
        result = list(
            call(
                functools.partial(apply_kernel, stage, 0 if last else 3),
                args,
                tuple(outs),
                scratch=(
                    pltpu.VMEM((levels * members, points), jnp.float32),
                    side_scratch,
                    level_scratch,
                    pltpu.VMEM((8 * RATIO, LANES), jnp.float32),
                    pltpu.VMEM((RATIO, points), jnp.float32),
                ),
                flops=int(1e9),
            )
        )
        new = {name: result.pop(0) for name in STATE_OUT[stage]}
        dots = result.pop(0)
        scalar = result.pop(0) if stage else jnp.zeros((8, LANES), jnp.float32)
        return new, dots, scalar, result

    parts = call(
        functools.partial(start_kernel, 3),
        (rhs, pert, weights),
        part_shapes,
        scratch=(level_scratch, side_scratch),
        flops=int(1e8),
    )
    state, dots, scalar = dict(r=rhs), None, None
    for stage in range(ITERS):
        pieces, dots = extend(parts, dots)
        new, dots, scalar, parts = apply(stage, pieces, dots, scalar, state)
        if stage == 1:
            state.update(s=state["w"], p=state["r"])
        state.update(new)

    dots = lax.all_to_all(dots, ("patch", "lev"), 0, 0, tiled=True)
    x, r = call(
        final_kernel,
        (dots, scalar, *(state[name] for name in "spxrw")),
        (grid_shape, grid_shape),
    )
    unfold = lambda a: jnp.swapaxes(a, -1, -2).reshape(levels, columns)
    return unfold(x), unfold(r)


def solution(mesh):
    in_specs = (
        P("lev", "patch"),
        P("lev", "patch"),
        P(None, "lev", "patch"),
        P("patch"),
        P("patch"),
        P(),
        P(),
    )
    out_specs = (P("lev", "patch"), P("lev", "patch"))
    return jax.shard_map(shards, mesh=mesh, in_specs=in_specs, out_specs=out_specs, check_vma=False)
```

```python
import functools

import jax
import jax.numpy as jnp
import numpy as np
from jax import lax
from jax.experimental import pallas as pl
from jax.experimental.pallas import tpu as pltpu
from jax.sharding import PartitionSpec as P

MEMBERS = 40
RATIO = 16
HALO = 128
ITERS = 4
LANES = 128
REACH = 2 * HALO
VMEM_LIMIT = 24 * 1024 * 1024
GROUP = LANES * RATIO
PAIR = 2 * LANES


def tap_blocks():
    reach = np.arange(HALO + 1)
    rough = 0.5 + ((97 * reach * reach + 31 * reach) % 257) / 256.0
    raw = (1.0 - reach / (2.0 * HALO)) * rough
    taps = raw / np.sqrt(2.0 * np.sum(raw**2) - raw[0] ** 2)
    rows, cols = np.arange(HALO)[:, None], np.arange(HALO)[None, :]
    blocks = []
    for shift in range(3):
        distance = np.abs(rows - cols + (1 - shift) * HALO)
        blocks.append(np.where(distance <= HALO, taps[np.minimum(distance, HALO)], 0.0))
    return blocks


def block_products():
    blocks = tap_blocks()
    return np.stack([np.stack([a.T @ b for b in blocks]) for a in blocks]).astype(np.float32)


def band_kernel(counts_ref, prod_ref, hi_ref, lo_ref):
    own_blocks = hi_ref.shape[1] // HALO
    edge = (0, own_blocks + 1)
    lane = lax.broadcasted_iota(jnp.int32, (HALO, HALO), 1)
    row = lax.broadcasted_iota(jnp.int32, (HALO, HALO), 0)
    crossing = {
        (0, 2): (counts_ref[0], False),
        (1, 1): (counts_ref[1], True),
        (own_blocks, own_blocks + 2): (counts_ref[1], False),
        (own_blocks + 1, own_blocks + 1): (counts_ref[2], True),
    }

    def keep(index, key):
        count, from_end = crossing[key]
        return (HALO - 1 - index if from_end else index) < count

    for source in range(own_blocks + 4):
        for target in range(2, own_blocks + 2):
            total = jnp.zeros((HALO, HALO), jnp.float32)
            for i in range(edge[0], edge[1] + 1):
                a, b = source - i, target - i
                if not (0 <= a < 3 and 0 <= b < 3):
                    continue
                term = prod_ref[a, b]
                if (i, source) in crossing:
                    term = jnp.where(keep(row, (i, source)), term, 0.0)
                if (i, target) in crossing:
                    term = jnp.where(keep(lane, (i, target)), term, 0.0)
                total = total + term
            hi = total.astype(jnp.bfloat16)
            at = (pl.ds(source * HALO, HALO), pl.ds((target - 2) * HALO, HALO))
            hi_ref[at] = hi
            lo_ref[at] = (total - hi.astype(jnp.float32)).astype(jnp.bfloat16)


def to_subgrid(pert_ref, field_ref, weight_ref, part_refs, level_ref, side_ref):
    levels, ratio, points = field_ref.shape
    members = pert_ref.shape[1] // ratio
    tiles = members // 8

    def one_level(level):
        for lane_tile in range(points // LANES):
            lanes = pl.ds(lane_tile * LANES, LANES)
            field = field_ref[level, :, lanes]
            for j in range(3):
                level_ref[j] = field * weight_ref[j, lane_tile]
            total = [[None] * tiles for _ in range(3)]
            for r in range(ratio):
                scale = [level_ref[j, pl.ds(r, 8, stride=0), :] for j in range(3)]
                for t in range(tiles):
                    pert = pert_ref[level, pl.ds(r * members + 8 * t, 8), lanes]
                    for j in range(3):
                        term = pert * scale[j]
                        total[j][t] = term if total[j][t] is None else total[j][t] + term
            for j in range(3):
                for t in range(tiles):
                    side_ref[j, pl.ds(8 * t, 8), lanes] = total[j][t]
        return (
            side_ref[1]
            + pltpu.roll(side_ref[0], points - 1, axis=1)
            + pltpu.roll(side_ref[2], 1, axis=1)
        )

    first = 0
    for ref in part_refs:
        count = ref.shape[0] // members

        def body(k, carry, ref=ref, first=first):
            rows = pl.ds(pl.multiple_of(k * members, 8), members)
            ref[rows, :] = one_level(first + k)
            return carry

        lax.fori_loop(0, count, body, 0)
        first += count


def from_subgrid(pert_ref, level, values, weight_ref, side_ref, sum_ref, out_ref):
    members, points = values.shape
    ratio = out_ref.shape[0]
    tiles = members // 8
    side_ref[0] = pltpu.roll(values, 1, axis=1)
    side_ref[1] = values
    side_ref[2] = pltpu.roll(values, points - 1, axis=1)
    for lane_tile in range(points // LANES):
        lanes = pl.ds(lane_tile * LANES, LANES)
        near = [[side_ref[j, pl.ds(8 * t, 8), lanes] for t in range(tiles)] for j in range(3)]
        for r in range(ratio):
            total = [None] * 3
            for t in range(tiles):
                pert = pert_ref[level, pl.ds(r * members + 8 * t, 8), lanes]
                for j in range(3):
                    term = pert * near[j][t]
                    total[j] = term if total[j] is None else total[j] + term
            mixed = None
            for j in range(3):
                term = total[j] * weight_ref[j, lane_tile, pl.ds(r, 8, stride=0), :]
                mixed = term if mixed is None else mixed + term
            sum_ref[pl.ds(8 * r, 8), :] = mixed
        result = sum_ref[pl.ds(0, ratio, stride=8), :]
        for k in range(1, 8):
            result = result + sum_ref[pl.ds(k, ratio, stride=8), :]
        out_ref[:, lanes] = result


def split(x):
    hi = x.astype(jnp.bfloat16)
    return hi, (x - hi.astype(jnp.float32)).astype(jnp.bfloat16)


def band_product(pieces, hi_ref, lo_ref, out_ref):
    halves = [split(ref[...]) for ref in pieces]
    for block in range(out_ref.shape[1] // REACH):
        cols = pl.ds(block * REACH, REACH)
        total = None
        for k in range(block, block + 3):
            hi, lo = halves[k]
            rows = pl.ds(k * REACH, REACH)
            for left, right_ref in ((hi, hi_ref), (lo, hi_ref), (hi, lo_ref)):
                term = jnp.dot(left, right_ref[rows, cols], preferred_element_type=jnp.float32)
                total = term if total is None else total + term
        out_ref[:, cols] = total


def sums(dots_ref):
    total = jnp.sum(dots_ref[...], axis=0)
    return total[0:1], total[1:2]


def step_sizes(stage, dots_ref, scalar_ref):
    gamma, delta = sums(dots_ref)
    if stage == 1:
        return gamma, gamma / delta, None
    beta = gamma / scalar_ref[0:1]
    alpha = gamma / (delta - beta * gamma / scalar_ref[1:2])
    return gamma, alpha, beta


STATE_IN = {0: "r", 1: "rw", 2: "zspxrw", 3: "zspxrw"}
STATE_OUT = {0: "w", 1: "zxrw", 2: "zspxrw", 3: "spxrw"}


def apply_kernel(stage, parts, *refs):
    refs = list(refs)
    take = lambda n: [refs.pop(0) for _ in range(n)]
    pieces = take(4)
    hi_ref, lo_ref, pert_ref, weight_ref, error_ref = take(5)
    dots_in, scalar_in = take(2) if stage else (None, None)
    state = dict(zip(STATE_IN[stage], take(len(STATE_IN[stage]))))
    new = dict(zip(STATE_OUT[stage], take(len(STATE_OUT[stage]))))
    (dots_out,) = take(1)
    (scalar_out,) = take(1) if stage else (None,)
    part_refs = take(parts)
    conv_ref, side_ref, level_ref, sum_ref, image_ref = refs

    levels, ratio, points = error_ref.shape
    members = pert_ref.shape[1] // ratio
    band_product(pieces, hi_ref, lo_ref, conv_ref)

    alpha = beta = None
    if stage:
        gamma, alpha, beta = step_sizes(stage, dots_in, scalar_in)
        scalar_out[0:1] = gamma
        scalar_out[1:2] = alpha
        alpha = jnp.concatenate([alpha] * (points // LANES), axis=1)
        if beta is not None:
            beta = jnp.concatenate([beta] * (points // LANES), axis=1)

    def one_level(level, carry):
        rows = pl.ds(pl.multiple_of(level * members, 8), members)
        from_subgrid(pert_ref, level, conv_ref[rows, :], weight_ref, side_ref, sum_ref, image_ref)
        mean = image_ref[...] * (1.0 / (MEMBERS - 1))
        r = state["r"][level]
        if stage == 0:
            w = error_ref[level] * r + mean
            new["w"][level] = w
        else:
            w = state["w"][level]
            z = error_ref[level] * w + mean
            s, p = w, r
            if stage > 1:
                z = z + beta * state["z"][level]
                s = s + beta * state["s"][level]
                p = p + beta * state["p"][level]
            x = alpha * p
            if stage > 1:
                x = x + state["x"][level]
            r = r - alpha * s
            w = w - alpha * z
            for name, value in dict(z=z, s=s, p=p, x=x, r=r, w=w).items():
                if name in new:
                    new[name][level] = value
        return carry[0] + r * r, carry[1] + r * w

    zero = jnp.zeros((ratio, points), jnp.float32)
    total = lax.fori_loop(0, levels, one_level, (zero, zero))
    partial = [jnp.broadcast_to(jnp.sum(t, keepdims=True), (1, LANES)) for t in total]
    partial = jnp.concatenate(partial, axis=0)
    dots_out[...] = jnp.broadcast_to(partial[None], dots_out.shape)
    if parts:
        to_subgrid(pert_ref, new["w"], weight_ref, part_refs, level_ref, side_ref)


def final_kernel(
    dots_ref, scalar_ref, s_ref, p_ref, x_ref, r_ref, w_ref, x_out, r_out, stack_ref
):
    levels, ratio, points = x_ref.shape
    _, alpha, beta = step_sizes(ITERS - 1, dots_ref, scalar_ref)
    exact = permutation(jnp.float32)
    rows = stack_ref.shape[0] // ratio
    stack_ref[...] = jnp.zeros_like(stack_ref)
    for group in range(points // LANES):
        lanes = pl.ds(group * LANES, LANES)
        for level in range(levels):
            s = w_ref[level, :, lanes] + beta * s_ref[level, :, lanes]
            p = r_ref[level, :, lanes] + beta * p_ref[level, :, lanes]
            x = x_ref[level, :, lanes] + alpha * p
            r = r_ref[level, :, lanes] - alpha * s
            stack_ref[pl.ds(level * ratio, ratio), :] = x
            stack_ref[pl.ds((8 + level) * ratio, ratio), :] = r
        halves = []
        for half in range(2):
            blocks = [stack_ref[pl.ds(half * 8 + k, rows, stride=ratio), :] for k in range(8)]
            halves.append(jnp.concatenate(exchange(blocks), axis=0))
        turned = jnp.dot(
            jnp.concatenate(halves, axis=1),
            exact,
            precision=lax.Precision.HIGHEST,
            preferred_element_type=jnp.float32,
        )
        for t in range(8):
            cols = pl.ds(group * GROUP + t * PAIR, PAIR)
            x_out[:, cols] = turned[t * rows : t * rows + levels]
            r_out[:, cols] = turned[t * rows + 8 : t * rows + 8 + levels]


def vertical_kernel(coupling_ref, below_ref, *refs):
    *own_refs, above_ref, left_ref, right_ref = refs
    where = []
    for ref in (below_ref, *own_refs, above_ref):
        for k in range(ref.shape[0] // MEMBERS):
            where.append((ref, k * MEMBERS))
    levels = len(where) - 4

    def body(t, carry):
        field = [ref[pl.ds(base + pl.multiple_of(t * 8, 8), 8), :] for ref, base in where]
        stepped = [
            field[l + 1] + coupling_ref[l] * (field[l] + field[l + 2]) for l in range(levels + 2)
        ]
        scaled = [coupling_ref[l] * stepped[l] for l in range(levels + 2)]
        for l in range(levels):
            value = stepped[l + 1] + (scaled[l] + scaled[l + 2])
            rows = pl.ds(l * MEMBERS + pl.multiple_of(t * 8, 8), 8)
            left_ref[rows, :] = value[:, :REACH]
            right_ref[rows, :] = value[:, value.shape[1] - REACH :]
        return carry

    lax.fori_loop(0, MEMBERS // 8, body, 0)


def exchange(blocks):
    lane = lax.broadcasted_iota(jnp.int32, blocks[0].shape, 1)
    blocks = list(blocks)
    for bit in (4, 2, 1):
        far = 16 * bit
        upper = (lane & far) != 0
        for k in range(8):
            if k & bit:
                continue
            a, b = blocks[k], blocks[k + bit]
            blocks[k] = jnp.where(upper, pltpu.roll(b, far, axis=1), a)
            blocks[k + bit] = jnp.where(upper, b, pltpu.roll(a, LANES - far, axis=1))
    return blocks


def permutation(dtype):
    row = lax.broadcasted_iota(jnp.int32, (PAIR, PAIR), 0)
    col = lax.broadcasted_iota(jnp.int32, (PAIR, PAIR), 1)
    return jnp.where((row % 16) * 16 + row // 16 == col, 1.0, 0.0).astype(dtype)


def start_kernel(
    parts, rhs_ref, error_ref, slot_ref, weight_ref, pert_ref, field_ref, error_out, weight_out, *refs
):
    pert_out, *refs = refs
    part_refs = refs[:parts]
    stack_ref, turn_ref, level_ref, side_ref = refs[parts:]
    levels, members, columns = pert_ref.shape
    ratio = RATIO

    stack_ref[...] = jnp.zeros_like(stack_ref)
    stack_ref[0:levels] = rhs_ref[...]
    stack_ref[8 : 8 + levels] = error_ref[...]
    weight = weight_ref[...]
    column = lax.broadcasted_iota(jnp.int32, weight.shape, 1)
    is_lower = slot_ref[...] < column // ratio
    stack_ref[16:17] = jnp.where(is_lower, weight, 0.0)
    stack_ref[17:18] = jnp.where(is_lower, 1.0 - weight, weight)
    stack_ref[18:19] = jnp.where(is_lower, 0.0, 1.0 - weight)
    exact = permutation(jnp.float32)
    rows = stack_ref.shape[0]
    for group in range(columns // GROUP):
        blocks = [stack_ref[:, pl.ds(group * GROUP + t * PAIR, PAIR)] for t in range(8)]
        turned = jnp.dot(
            jnp.concatenate(blocks, axis=0),
            exact,
            precision=lax.Precision.HIGHEST,
            preferred_element_type=jnp.float32,
        )
        for half in range(2):
            lanes = slice(half * LANES, (half + 1) * LANES)
            out = exchange([turned[t * rows : (t + 1) * rows, lanes] for t in range(8)])
            for k in range(8):
                turn_ref[pl.ds((half * 8 + k) * rows, rows), :] = out[k]
        point = pl.ds(group * LANES, LANES)
        picked = lambda f: turn_ref[pl.ds(f, ratio, stride=rows), :]
        for level in range(levels):
            field_ref[level, :, point] = picked(level)
            error_out[level, :, point] = picked(8 + level)
        for j in range(3):
            weight_out[j, group] = picked(16 + j)

    turn = permutation(jnp.bfloat16)

    def one_level(level, carry):
        for group in range(columns // GROUP):
            blocks = [
                pert_ref[level, :, pl.ds(group * GROUP + t * PAIR, PAIR)].astype(jnp.float32)
                for t in range(8)
            ]
            stacked = jnp.concatenate(blocks, axis=0).astype(jnp.bfloat16)
            turned = jnp.dot(stacked, turn, preferred_element_type=jnp.float32)
            for half in range(2):
                for m in range(0, members, 8):
                    lanes = slice(half * LANES, (half + 1) * LANES)
                    out = exchange(
                        [turned[t * members + m : t * members + m + 8, lanes] for t in range(8)]
                    )
                    for k in range(8):
                        at = pl.ds((half * 8 + k) * members + m, 8)
                        pert_out[level, at, pl.ds(group * LANES, LANES)] = out[k]
        return carry

    lax.fori_loop(0, levels, one_level, 0)
    to_subgrid(pert_out, field_ref, weight_out, part_refs, level_ref, side_ref)


def whole():
    return pl.BlockSpec(memory_space=pltpu.VMEM)


def scalars():
    return pl.BlockSpec(memory_space=pltpu.SMEM)


def call(kernel, args, out_shape, scratch=(), flops=0, in_specs=None):
    size = sum(np.prod(a.shape) * a.dtype.itemsize for a in args)
    return pl.pallas_call(
        kernel,
        in_specs=in_specs or [whole()] * len(args),
        out_specs=jax.tree.map(lambda _: whole(), out_shape),
        out_shape=out_shape,
        scratch_shapes=list(scratch),
        compiler_params=pltpu.CompilerParams(vmem_limit_bytes=VMEM_LIMIT),
        cost_estimate=pl.CostEstimate(flops=flops, bytes_accessed=int(size), transcendentals=0),
    )(*args)


def f32(*shape):
    return jax.ShapeDtypeStruct(shape, jnp.float32)


def shift(block, axis, step, periodic):
    count = lax.axis_size(axis)
    pairs = [(i, (i + step) % count) for i in range(count) if periodic or 0 <= i + step < count]
    return lax.ppermute(block, axis, pairs)


def shards(
    increment_rhs,
    error_variance,
    perturbations,
    interp_slot,
    interp_weight,
    halo_rows,
    vertical_coupling,
):
    members, levels, columns = perturbations.shape
    points = columns // RATIO
    devices = lax.axis_size("patch") * lax.axis_size("lev")

    patch, patches = lax.axis_index("patch"), lax.axis_size("patch")
    near = (patch + jnp.array([patches - 1, 0, 1])) % patches
    extended = points + 2 * REACH
    band_hi, band_lo = call(
        band_kernel,
        (halo_rows[near], jnp.asarray(block_products())),
        (jax.ShapeDtypeStruct((extended, points), jnp.bfloat16),) * 2,
        in_specs=[scalars(), whole()],
    )
    first_level = lax.axis_index("lev") * levels
    coupling = lax.dynamic_slice(jnp.pad(vertical_coupling, 1), (first_level,), (levels + 2,))

    part_levels = (2, levels - 4, 2)
    part_shapes = tuple(f32(n * members, points) for n in part_levels)
    level_scratch = pltpu.VMEM((3, RATIO, LANES), jnp.float32)
    side_scratch = pltpu.VMEM((3, members, points), jnp.float32)
    grid_shape = f32(levels, RATIO, points)

    def extend(parts, dots):
        low, middle, high = parts
        from_below = shift(high, "lev", 1, False)
        from_above = shift(low, "lev", -1, False)
        half = f32(levels * members, REACH)
        left, right = call(
            vertical_kernel,
            (coupling, from_below, low, middle, high, from_above),
            (half, half),
            in_specs=[scalars()] + [whole()] * 5,
        )
        if dots is not None:
            dots, left, right = lax.optimization_barrier((dots, left, right))
        from_left = shift(right, "patch", 1, True)
        from_right = shift(left, "patch", -1, True)
        if dots is not None:
            dots = lax.all_to_all(dots, ("patch", "lev"), 0, 0, tiled=True)
        return (from_left, left, right, from_right), dots

    def apply(stage, pieces, dots, scalar, state):
        outs = [grid_shape] * len(STATE_OUT[stage]) + [f32(devices, 2, LANES)]
        outs += [f32(8, LANES)] if stage else []
        last = stage == ITERS - 1
        outs += [] if last else list(part_shapes)
        args = [*pieces, band_hi, band_lo, pert, weights, error]
        args += [dots, scalar] if stage else []
        args += [state[name] for name in STATE_IN[stage]]
        result = list(
            call(
                functools.partial(apply_kernel, stage, 0 if last else 3),
                args,
                tuple(outs),
                scratch=(
                    pltpu.VMEM((levels * members, points), jnp.float32),
                    side_scratch,
                    level_scratch,
                    pltpu.VMEM((8 * RATIO, LANES), jnp.float32),
                    pltpu.VMEM((RATIO, points), jnp.float32),
                ),
                flops=int(1e9),
            )
        )
        new = {name: result.pop(0) for name in STATE_OUT[stage]}
        dots = result.pop(0)
        scalar = result.pop(0) if stage else jnp.zeros((8, LANES), jnp.float32)
        return new, dots, scalar, result

    rhs, error, weights, pert, *parts = call(
        functools.partial(start_kernel, 3),
        (
            increment_rhs,
            error_variance,
            interp_slot[None],
            interp_weight[None],
            perturbations.transpose(1, 0, 2),
        ),
        (
            grid_shape,
            grid_shape,
            f32(3, points // LANES, RATIO, LANES),
            f32(levels, RATIO * members, points),
            *part_shapes,
        ),
        scratch=(
            pltpu.VMEM((24, columns), jnp.float32),
            pltpu.VMEM((24 * RATIO, LANES), jnp.float32),
            level_scratch,
            side_scratch,
        ),
        flops=int(1e8),
    )
    state, dots, scalar = dict(r=rhs), None, None
    for stage in range(ITERS):
        pieces, dots = extend(parts, dots)
        new, dots, scalar, parts = apply(stage, pieces, dots, scalar, state)
        if stage == 1:
            state.update(s=state["w"], p=state["r"])
        state.update(new)

    dots = lax.all_to_all(dots, ("patch", "lev"), 0, 0, tiled=True)
    return call(
        final_kernel,
        (dots, scalar, *(state[name] for name in "spxrw")),
        (f32(levels, columns),) * 2,
        scratch=(pltpu.VMEM((16 * RATIO, LANES), jnp.float32),),
    )


def solution(mesh):
    in_specs = (
        P("lev", "patch"),
        P("lev", "patch"),
        P(None, "lev", "patch"),
        P("patch"),
        P("patch"),
        P(),
        P(),
    )
    out_specs = (P("lev", "patch"), P("lev", "patch"))
    return jax.shard_map(shards, mesh=mesh, in_specs=in_specs, out_specs=out_specs, check_vma=False)
```

```python
import functools

import jax
import jax.numpy as jnp
import numpy as np
from jax import lax
from jax.experimental import pallas as pl
from jax.experimental.pallas import tpu as pltpu
from jax.sharding import PartitionSpec as P

MEMBERS = 40
RATIO = 16
HALO = 128
ITERS = 4
LANES = 128
REACH = 2 * HALO
VMEM_LIMIT = 24 * 1024 * 1024
GROUP = LANES * RATIO
PAIR = 2 * LANES


def tap_blocks():
    reach = np.arange(HALO + 1)
    rough = 0.5 + ((97 * reach * reach + 31 * reach) % 257) / 256.0
    raw = (1.0 - reach / (2.0 * HALO)) * rough
    taps = raw / np.sqrt(2.0 * np.sum(raw**2) - raw[0] ** 2)
    rows, cols = np.arange(HALO)[:, None], np.arange(HALO)[None, :]
    blocks = []
    for shift in range(3):
        distance = np.abs(rows - cols + (1 - shift) * HALO)
        blocks.append(np.where(distance <= HALO, taps[np.minimum(distance, HALO)], 0.0))
    return blocks


def block_products():
    blocks = tap_blocks()
    return np.stack([np.stack([a.T @ b for b in blocks]) for a in blocks]).astype(np.float32)


def band_kernel(halo_ref, prod_ref, hi_ref, lo_ref):
    patch, patches = lax.axis_index("patch"), lax.axis_size("patch")
    counts = [halo_ref[lax.rem(patch + patches + step, patches)] for step in (-1, 0, 1)]
    own_blocks = hi_ref.shape[1] // HALO
    edge = (0, own_blocks + 1)
    lane = lax.broadcasted_iota(jnp.int32, (HALO, HALO), 1)
    row = lax.broadcasted_iota(jnp.int32, (HALO, HALO), 0)
    crossing = {
        (0, 2): (counts[0], False),
        (1, 1): (counts[1], True),
        (own_blocks, own_blocks + 2): (counts[1], False),
        (own_blocks + 1, own_blocks + 1): (counts[2], True),
    }

    def keep(index, key):
        count, from_end = crossing[key]
        return (HALO - 1 - index if from_end else index) < count

    for source in range(own_blocks + 4):
        for target in range(2, own_blocks + 2):
            total = jnp.zeros((HALO, HALO), jnp.float32)
            for i in range(edge[0], edge[1] + 1):
                a, b = source - i, target - i
                if not (0 <= a < 3 and 0 <= b < 3):
                    continue
                term = prod_ref[a, b]
                if (i, source) in crossing:
                    term = jnp.where(keep(row, (i, source)), term, 0.0)
                if (i, target) in crossing:
                    term = jnp.where(keep(lane, (i, target)), term, 0.0)
                total = total + term
            hi = total.astype(jnp.bfloat16)
            at = (pl.ds(source * HALO, HALO), pl.ds((target - 2) * HALO, HALO))
            hi_ref[at] = hi
            lo_ref[at] = (total - hi.astype(jnp.float32)).astype(jnp.bfloat16)


def to_subgrid(pert_ref, field_ref, weight_ref, part_refs, level_ref, side_ref):
    levels, ratio, points = field_ref.shape
    members = pert_ref.shape[1] // ratio
    tiles = members // 8

    def one_level(level):
        for lane_tile in range(points // LANES):
            lanes = pl.ds(lane_tile * LANES, LANES)
            field = field_ref[level, :, lanes]
            for j in range(3):
                level_ref[j] = field * weight_ref[j, lane_tile]
            total = [[None] * tiles for _ in range(3)]
            for r in range(ratio):
                scale = [level_ref[j, pl.ds(r, 8, stride=0), :] for j in range(3)]
                for t in range(tiles):
                    pert = pert_ref[level, pl.ds(r * members + 8 * t, 8), lanes]
                    for j in range(3):
                        term = pert * scale[j]
                        total[j][t] = term if total[j][t] is None else total[j][t] + term
            for j in range(3):
                for t in range(tiles):
                    side_ref[j, pl.ds(8 * t, 8), lanes] = total[j][t]
        return (
            side_ref[1]
            + pltpu.roll(side_ref[0], points - 1, axis=1)
            + pltpu.roll(side_ref[2], 1, axis=1)
        )

    first = 0
    for ref in part_refs:
        count = ref.shape[0] // members

        def body(k, carry, ref=ref, first=first):
            rows = pl.ds(pl.multiple_of(k * members, 8), members)
            ref[rows, :] = one_level(first + k)
            return carry

        lax.fori_loop(0, count, body, 0)
        first += count


def from_subgrid(pert_ref, level, values, weight_ref, side_ref, sum_ref, out_ref):
    members, points = values.shape
    ratio = out_ref.shape[0]
    tiles = members // 8
    side_ref[0] = pltpu.roll(values, 1, axis=1)
    side_ref[1] = values
    side_ref[2] = pltpu.roll(values, points - 1, axis=1)
    for lane_tile in range(points // LANES):
        lanes = pl.ds(lane_tile * LANES, LANES)
        near = [[side_ref[j, pl.ds(8 * t, 8), lanes] for t in range(tiles)] for j in range(3)]
        for r in range(ratio):
            total = [None] * 3
            for t in range(tiles):
                pert = pert_ref[level, pl.ds(r * members + 8 * t, 8), lanes]
                for j in range(3):
                    term = pert * near[j][t]
                    total[j] = term if total[j] is None else total[j] + term
            mixed = None
            for j in range(3):
                term = total[j] * weight_ref[j, lane_tile, pl.ds(r, 8, stride=0), :]
                mixed = term if mixed is None else mixed + term
            sum_ref[pl.ds(8 * r, 8), :] = mixed
        result = sum_ref[pl.ds(0, ratio, stride=8), :]
        for k in range(1, 8):
            result = result + sum_ref[pl.ds(k, ratio, stride=8), :]
        out_ref[:, lanes] = result


def split(x):
    hi = x.astype(jnp.bfloat16)
    return hi, (x - hi.astype(jnp.float32)).astype(jnp.bfloat16)


def band_product(pieces, hi_ref, lo_ref, out_ref):
    halves = [split(ref[...]) for ref in pieces]
    for block in range(out_ref.shape[1] // REACH):
        cols = pl.ds(block * REACH, REACH)
        total = None
        for k in range(block, block + 3):
            hi, lo = halves[k]
            rows = pl.ds(k * REACH, REACH)
            for left, right_ref in ((hi, hi_ref), (lo, hi_ref), (hi, lo_ref)):
                term = jnp.dot(left, right_ref[rows, cols], preferred_element_type=jnp.float32)
                total = term if total is None else total + term
        out_ref[:, cols] = total


def sums(dots_ref):
    total = jnp.sum(dots_ref[...], axis=0)
    return total[0:1], total[1:2]


def step_sizes(stage, dots_ref, scalar_ref):
    gamma, delta = sums(dots_ref)
    if stage == 1:
        return gamma, gamma / delta, None
    beta = gamma / scalar_ref[0:1]
    alpha = gamma / (delta - beta * gamma / scalar_ref[1:2])
    return gamma, alpha, beta


STATE_IN = {0: "r", 1: "rw", 2: "zspxrw", 3: "zspxrw"}
STATE_OUT = {0: "w", 1: "zxrw", 2: "zspxrw", 3: "spxrw"}


def apply_kernel(stage, parts, *refs):
    refs = list(refs)
    take = lambda n: [refs.pop(0) for _ in range(n)]
    pieces = take(4)
    hi_ref, lo_ref, pert_ref, weight_ref, error_ref = take(5)
    dots_in, scalar_in = take(2) if stage else (None, None)
    state = dict(zip(STATE_IN[stage], take(len(STATE_IN[stage]))))
    new = dict(zip(STATE_OUT[stage], take(len(STATE_OUT[stage]))))
    (dots_out,) = take(1)
    (scalar_out,) = take(1) if stage else (None,)
    part_refs = take(parts)
    conv_ref, side_ref, level_ref, sum_ref, image_ref = refs

    levels, ratio, points = error_ref.shape
    members = pert_ref.shape[1] // ratio
    band_product(pieces, hi_ref, lo_ref, conv_ref)

    alpha = beta = None
    if stage:
        gamma, alpha, beta = step_sizes(stage, dots_in, scalar_in)
        scalar_out[0:1] = gamma
        scalar_out[1:2] = alpha
        alpha = jnp.concatenate([alpha] * (points // LANES), axis=1)
        if beta is not None:
            beta = jnp.concatenate([beta] * (points // LANES), axis=1)

    def one_level(level, carry):
        rows = pl.ds(pl.multiple_of(level * members, 8), members)
        from_subgrid(pert_ref, level, conv_ref[rows, :], weight_ref, side_ref, sum_ref, image_ref)
        mean = image_ref[...] * (1.0 / (MEMBERS - 1))
        r = state["r"][level]
        if stage == 0:
            w = error_ref[level] * r + mean
            new["w"][level] = w
        else:
            w = state["w"][level]
            z = error_ref[level] * w + mean
            s, p = w, r
            if stage > 1:
                z = z + beta * state["z"][level]
                s = s + beta * state["s"][level]
                p = p + beta * state["p"][level]
            x = alpha * p
            if stage > 1:
                x = x + state["x"][level]
            r = r - alpha * s
            w = w - alpha * z
            for name, value in dict(z=z, s=s, p=p, x=x, r=r, w=w).items():
                if name in new:
                    new[name][level] = value
        return carry[0] + r * r, carry[1] + r * w

    zero = jnp.zeros((ratio, points), jnp.float32)
    total = lax.fori_loop(0, levels, one_level, (zero, zero))
    partial = [jnp.broadcast_to(jnp.sum(t, keepdims=True), (1, LANES)) for t in total]
    partial = jnp.concatenate(partial, axis=0)
    dots_out[...] = jnp.broadcast_to(partial[None], dots_out.shape)
    if parts:
        to_subgrid(pert_ref, new["w"], weight_ref, part_refs, level_ref, side_ref)


def final_kernel(
    dots_ref, scalar_ref, s_ref, p_ref, x_ref, r_ref, w_ref, x_out, r_out, stack_ref
):
    levels, ratio, points = x_ref.shape
    _, alpha, beta = step_sizes(ITERS - 1, dots_ref, scalar_ref)
    matrices = permutations(transposed=True)
    rows = stack_ref.shape[0] // ratio
    stack_ref[...] = jnp.zeros_like(stack_ref)
    for group in range(points // LANES):
        lanes = pl.ds(group * LANES, LANES)
        for level in range(levels):
            s = w_ref[level, :, lanes] + beta * s_ref[level, :, lanes]
            p = r_ref[level, :, lanes] + beta * p_ref[level, :, lanes]
            x = x_ref[level, :, lanes] + alpha * p
            r = r_ref[level, :, lanes] - alpha * s
            stack_ref[pl.ds(level * ratio, ratio), :] = x
            stack_ref[pl.ds((8 + level) * ratio, ratio), :] = r
        tiles = [
            three_terms(stack_ref[pl.ds(r, rows, stride=ratio), :]) for r in range(ratio)
        ]
        for t, tile in enumerate(turn_back(tiles, matrices)):
            tile = sum_of_terms(tile)
            cols = pl.ds(group * GROUP + t * LANES, LANES)
            x_out[:, cols] = tile[:levels]
            r_out[:, cols] = tile[8 : 8 + levels]


def vertical_kernel(coupling_ref, below_ref, *refs):
    *own_refs, above_ref, left_ref, right_ref = refs
    where = []
    for ref in (below_ref, *own_refs, above_ref):
        for k in range(ref.shape[0] // MEMBERS):
            where.append((ref, k * MEMBERS))
    levels = len(where) - 4
    first = lax.axis_index("lev") * levels - 1
    all_levels = coupling_ref.shape[0]
    coupling = []
    for k in range(levels + 2):
        at = jnp.clip(first + k, 0, all_levels - 1)
        coupling.append(jnp.where(at == first + k, coupling_ref[at], 0.0))

    def body(t, carry):
        field = [ref[pl.ds(base + pl.multiple_of(t * 8, 8), 8), :] for ref, base in where]
        stepped = [
            field[l + 1] + coupling[l] * (field[l] + field[l + 2]) for l in range(levels + 2)
        ]
        scaled = [coupling[l] * stepped[l] for l in range(levels + 2)]
        for l in range(levels):
            value = stepped[l + 1] + (scaled[l] + scaled[l + 2])
            rows = pl.ds(l * MEMBERS + pl.multiple_of(t * 8, 8), 8)
            left_ref[rows, :] = value[:, :REACH]
            right_ref[rows, :] = value[:, value.shape[1] - REACH :]
        return carry

    lax.fori_loop(0, MEMBERS // 8, body, 0)


def permutations(transposed=False):
    row = lax.broadcasted_iota(jnp.int32, (PAIR, PAIR), 1 if transposed else 0)
    col = lax.broadcasted_iota(jnp.int32, (PAIR, PAIR), 0 if transposed else 1)
    targets = [(row % 16) * 16 + row // 16]
    for kept in (2, 1, 0):
        low = 6 - kept
        new, out = row // 128, (row // 64) % 2
        middle, rest = (row % 64) >> low, row % (1 << low)
        targets.append(out * 128 + (middle << (low + 1)) + (new << low) + rest)
    return [jnp.where(target == col, 1.0, 0.0).astype(jnp.bfloat16) for target in targets]


def turn(tiles, matrices):
    rows = tiles[0].shape[0]
    for bit, matrix in zip((1, 2, 4, 8), matrices):
        pairs = [(k, k + bit) for k in range(16) if not k & bit]
        stacked = [jnp.concatenate([tiles[k] for k in pair], axis=1) for pair in pairs]
        stacked = jnp.concatenate(stacked, axis=0).astype(jnp.bfloat16)
        turned = jnp.dot(stacked, matrix, preferred_element_type=jnp.float32)
        tiles = [None] * 16
        for i, pair in enumerate(pairs):
            for half, k in enumerate(pair):
                lanes = slice(half * LANES, (half + 1) * LANES)
                tiles[k] = turned[i * rows : (i + 1) * rows, lanes]
    return [tiles[sum(((r >> i) & 1) << (3 - i) for i in range(4))] for r in range(16)]


def turn_back(tiles, matrices):
    rows = tiles[0].shape[0]
    tiles = [tiles[sum(((r >> i) & 1) << (3 - i) for i in range(4))] for r in range(16)]
    for bit, matrix in reversed(list(zip((1, 2, 4, 8), matrices))):
        pairs = [(k, k + bit) for k in range(16) if not k & bit]
        stacked = [jnp.concatenate([tiles[k] for k in pair], axis=1) for pair in pairs]
        stacked = jnp.concatenate(stacked, axis=0).astype(jnp.bfloat16)
        turned = jnp.dot(stacked, matrix, preferred_element_type=jnp.float32)
        tiles = [None] * 16
        for i, pair in enumerate(pairs):
            for half, k in enumerate(pair):
                lanes = slice(half * LANES, (half + 1) * LANES)
                tiles[k] = turned[i * rows : (i + 1) * rows, lanes]
    return tiles


def three_terms(x):
    hi = x.astype(jnp.bfloat16).astype(jnp.float32)
    rest = x - hi
    middle = rest.astype(jnp.bfloat16).astype(jnp.float32)
    return jnp.concatenate([hi, middle, rest - middle], axis=0)


def sum_of_terms(x):
    rows = x.shape[0] // 3
    return x[:rows] + (x[rows : 2 * rows] + x[2 * rows :])


def start_kernel(
    parts, rhs_ref, error_ref, slot_ref, weight_ref, pert_ref, field_ref, error_out, weight_out, *refs
):
    pert_out, *refs = refs
    part_refs = refs[:parts]
    stack_ref, turn_ref, fetched_ref, level_ref, side_ref, sems = refs[parts:]
    levels, members, columns = pert_ref.shape
    ratio = RATIO
    copies = [
        pltpu.make_async_copy(pert_ref.at[l], fetched_ref.at[l], sems.at[l]) for l in range(levels)
    ]
    for copy in copies:
        copy.start()

    stack_ref[...] = jnp.zeros_like(stack_ref)
    stack_ref[0:levels] = rhs_ref[...]
    stack_ref[8 : 8 + levels] = error_ref[...]
    weight = weight_ref[...]
    column = lax.broadcasted_iota(jnp.int32, weight.shape, 1)
    is_lower = slot_ref[...] < column // ratio
    stack_ref[16:17] = jnp.where(is_lower, weight, 0.0)
    stack_ref[17:18] = jnp.where(is_lower, 1.0 - weight, weight)
    stack_ref[18:19] = jnp.where(is_lower, 0.0, 1.0 - weight)
    matrices = permutations()
    rows = stack_ref.shape[0]
    for group in range(columns // GROUP):
        tiles = [
            three_terms(stack_ref[:, pl.ds(group * GROUP + t * LANES, LANES)]) for t in range(16)
        ]
        for r, tile in enumerate(turn(tiles, matrices)):
            turn_ref[pl.ds(r * rows, rows), :] = sum_of_terms(tile)
        point = pl.ds(group * LANES, LANES)
        picked = lambda f: turn_ref[pl.ds(f, ratio, stride=rows), :]
        for level in range(levels):
            field_ref[level, :, point] = picked(level)
            error_out[level, :, point] = picked(8 + level)
        for j in range(3):
            weight_out[j, group] = picked(16 + j)

    for level in range(levels):
        copies[level].wait()

        def one_group(group, carry, level=level):
            tiles = []
            for t in range(16):
                cols = pl.ds(pl.multiple_of(group * GROUP + t * LANES, LANES), LANES)
                tiles.append(fetched_ref[level, :, cols].astype(jnp.float32))
            lanes = pl.ds(pl.multiple_of(group * LANES, LANES), LANES)
            for r, tile in enumerate(turn(tiles, matrices)):
                pert_out[level, pl.ds(r * members, members), lanes] = tile
            return carry

        lax.fori_loop(0, columns // GROUP, one_group, 0)
    to_subgrid(pert_out, field_ref, weight_out, part_refs, level_ref, side_ref)


def whole():
    return pl.BlockSpec(memory_space=pltpu.VMEM)


def scalars():
    return pl.BlockSpec(memory_space=pltpu.SMEM)


def call(kernel, args, out_shape, scratch=(), flops=0, in_specs=None):
    size = sum(np.prod(a.shape) * a.dtype.itemsize for a in args)
    return pl.pallas_call(
        kernel,
        in_specs=in_specs or [whole()] * len(args),
        out_specs=jax.tree.map(lambda _: whole(), out_shape),
        out_shape=out_shape,
        scratch_shapes=list(scratch),
        compiler_params=pltpu.CompilerParams(vmem_limit_bytes=VMEM_LIMIT),
        cost_estimate=pl.CostEstimate(flops=flops, bytes_accessed=int(size), transcendentals=0),
    )(*args)


def f32(*shape):
    return jax.ShapeDtypeStruct(shape, jnp.float32)


def shift(block, axis, step, periodic):
    count = lax.axis_size(axis)
    pairs = [(i, (i + step) % count) for i in range(count) if periodic or 0 <= i + step < count]
    return lax.ppermute(block, axis, pairs)


def shards(
    increment_rhs,
    error_variance,
    perturbations,
    interp_slot,
    interp_weight,
    halo_rows,
    vertical_coupling,
):
    members, levels, columns = perturbations.shape
    points = columns // RATIO
    devices = lax.axis_size("patch") * lax.axis_size("lev")

    extended = points + 2 * REACH
    band_hi, band_lo = call(
        band_kernel,
        (halo_rows, jnp.asarray(block_products())),
        (jax.ShapeDtypeStruct((extended, points), jnp.bfloat16),) * 2,
        in_specs=[scalars(), whole()],
    )
    part_levels = (2, levels - 4, 2)
    part_shapes = tuple(f32(n * members, points) for n in part_levels)
    level_scratch = pltpu.VMEM((3, RATIO, LANES), jnp.float32)
    side_scratch = pltpu.VMEM((3, members, points), jnp.float32)
    grid_shape = f32(levels, RATIO, points)

    def extend(parts, dots):
        low, middle, high = parts
        from_below = shift(high, "lev", 1, False)
        from_above = shift(low, "lev", -1, False)
        half = f32(levels * members, REACH)
        left, right = call(
            vertical_kernel,
            (vertical_coupling, from_below, low, middle, high, from_above),
            (half, half),
            in_specs=[scalars()] + [whole()] * 5,
        )
        if dots is not None:
            dots, left, right = lax.optimization_barrier((dots, left, right))
        from_left = shift(right, "patch", 1, True)
        from_right = shift(left, "patch", -1, True)
        if dots is not None:
            dots = lax.all_to_all(dots, ("patch", "lev"), 0, 0, tiled=True)
        return (from_left, left, right, from_right), dots

    def apply(stage, pieces, dots, scalar, state):
        outs = [grid_shape] * len(STATE_OUT[stage]) + [f32(devices, 2, LANES)]
        outs += [f32(8, LANES)] if stage else []
        last = stage == ITERS - 1
        outs += [] if last else list(part_shapes)
        args = [*pieces, band_hi, band_lo, pert, weights, error]
        args += [dots, scalar] if stage else []
        args += [state[name] for name in STATE_IN[stage]]
        result = list(
            call(
                functools.partial(apply_kernel, stage, 0 if last else 3),
                args,
                tuple(outs),
                scratch=(
                    pltpu.VMEM((levels * members, points), jnp.float32),
                    side_scratch,
                    level_scratch,
                    pltpu.VMEM((8 * RATIO, LANES), jnp.float32),
                    pltpu.VMEM((RATIO, points), jnp.float32),
                ),
                flops=int(1e9),
            )
        )
        new = {name: result.pop(0) for name in STATE_OUT[stage]}
        dots = result.pop(0)
        scalar = result.pop(0) if stage else jnp.zeros((8, LANES), jnp.float32)
        return new, dots, scalar, result

    rhs, error, weights, pert, *parts = call(
        functools.partial(start_kernel, 3),
        (
            increment_rhs,
            error_variance,
            interp_slot[None],
            interp_weight[None],
            perturbations.transpose(1, 0, 2),
        ),
        (
            grid_shape,
            grid_shape,
            f32(3, points // LANES, RATIO, LANES),
            f32(levels, RATIO * members, points),
            *part_shapes,
        ),
        scratch=(
            pltpu.VMEM((24, columns), jnp.float32),
            pltpu.VMEM((24 * RATIO, LANES), jnp.float32),
            pltpu.VMEM((levels, members, columns), jnp.bfloat16),
            level_scratch,
            side_scratch,
            pltpu.SemaphoreType.DMA((levels,)),
        ),
        flops=int(1e8),
        in_specs=[whole()] * 4 + [pl.BlockSpec(memory_space=pl.ANY)],
    )
    state, dots, scalar = dict(r=rhs), None, None
    for stage in range(ITERS):
        pieces, dots = extend(parts, dots)
        new, dots, scalar, parts = apply(stage, pieces, dots, scalar, state)
        if stage == 1:
            state.update(s=state["w"], p=state["r"])
        state.update(new)

    dots = lax.all_to_all(dots, ("patch", "lev"), 0, 0, tiled=True)
    return call(
        final_kernel,
        (dots, scalar, *(state[name] for name in "spxrw")),
        (f32(levels, columns),) * 2,
        scratch=(pltpu.VMEM((16 * RATIO, LANES), jnp.float32),),
    )


def solution(mesh):
    in_specs = (
        P("lev", "patch"),
        P("lev", "patch"),
        P(None, "lev", "patch"),
        P("patch"),
        P("patch"),
        P(),
        P(),
    )
    out_specs = (P("lev", "patch"), P("lev", "patch"))
    return jax.shard_map(shards, mesh=mesh, in_specs=in_specs, out_specs=out_specs, check_vma=False)
```

```python
import functools

import jax
import jax.numpy as jnp
import numpy as np
from jax import lax
from jax.experimental import pallas as pl
from jax.experimental.pallas import tpu as pltpu
from jax.sharding import PartitionSpec as P

MEMBERS = 40
RATIO = 16
HALO = 128
ITERS = 4
LANES = 128
REACH = 2 * HALO
VMEM_LIMIT = 24 * 1024 * 1024
GROUP = LANES * RATIO
PAIR = 2 * LANES


def tap_blocks():
    reach = np.arange(HALO + 1)
    rough = 0.5 + ((97 * reach * reach + 31 * reach) % 257) / 256.0
    raw = (1.0 - reach / (2.0 * HALO)) * rough
    taps = raw / np.sqrt(2.0 * np.sum(raw**2) - raw[0] ** 2)
    rows, cols = np.arange(HALO)[:, None], np.arange(HALO)[None, :]
    blocks = []
    for shift in range(3):
        distance = np.abs(rows - cols + (1 - shift) * HALO)
        blocks.append(np.where(distance <= HALO, taps[np.minimum(distance, HALO)], 0.0))
    return blocks


def block_products():
    blocks = tap_blocks()
    return np.stack([np.stack([a.T @ b for b in blocks]) for a in blocks]).astype(np.float32)


def band_kernel(halo_ref, prod_ref, hi_ref, lo_ref):
    patch, patches = lax.axis_index("patch"), lax.axis_size("patch")
    counts = [halo_ref[lax.rem(patch + patches + step, patches)] for step in (-1, 0, 1)]
    own_blocks = hi_ref.shape[1] // HALO
    edge = (0, own_blocks + 1)
    lane = lax.broadcasted_iota(jnp.int32, (HALO, HALO), 1)
    row = lax.broadcasted_iota(jnp.int32, (HALO, HALO), 0)
    crossing = {
        (0, 2): (counts[0], False),
        (1, 1): (counts[1], True),
        (own_blocks, own_blocks + 2): (counts[1], False),
        (own_blocks + 1, own_blocks + 1): (counts[2], True),
    }

    def keep(index, key):
        count, from_end = crossing[key]
        return (HALO - 1 - index if from_end else index) < count

    for source in range(own_blocks + 4):
        for target in range(2, own_blocks + 2):
            total = jnp.zeros((HALO, HALO), jnp.float32)
            for i in range(edge[0], edge[1] + 1):
                a, b = source - i, target - i
                if not (0 <= a < 3 and 0 <= b < 3):
                    continue
                term = prod_ref[a, b]
                if (i, source) in crossing:
                    term = jnp.where(keep(row, (i, source)), term, 0.0)
                if (i, target) in crossing:
                    term = jnp.where(keep(lane, (i, target)), term, 0.0)
                total = total + term
            hi = total.astype(jnp.bfloat16)
            at = (pl.ds(source * HALO, HALO), pl.ds((target - 2) * HALO, HALO))
            hi_ref[at] = hi
            lo_ref[at] = (total - hi.astype(jnp.float32)).astype(jnp.bfloat16)


def to_subgrid(pert_ref, field_ref, weight_ref, part_refs, level_ref, side_ref):
    levels, ratio, points = field_ref.shape
    members = pert_ref.shape[1] // ratio
    tiles = members // 8

    def one_level(level):
        for lane_tile in range(points // LANES):
            lanes = pl.ds(lane_tile * LANES, LANES)
            field = field_ref[level, :, lanes]
            for j in range(3):
                level_ref[j] = field * weight_ref[j, lane_tile]
            total = [[None] * tiles for _ in range(3)]
            for r in range(ratio):
                scale = [level_ref[j, pl.ds(r, 8, stride=0), :] for j in range(3)]
                for t in range(tiles):
                    pert = pert_ref[level, pl.ds(r * members + 8 * t, 8), lanes]
                    for j in range(3):
                        term = pert * scale[j]
                        total[j][t] = term if total[j][t] is None else total[j][t] + term
            for j in range(3):
                for t in range(tiles):
                    side_ref[j, pl.ds(8 * t, 8), lanes] = total[j][t]
        return (
            side_ref[1]
            + pltpu.roll(side_ref[0], points - 1, axis=1)
            + pltpu.roll(side_ref[2], 1, axis=1)
        )

    first = 0
    for ref in part_refs:
        count = ref.shape[0] // members

        def body(k, carry, ref=ref, first=first):
            rows = pl.ds(pl.multiple_of(k * members, 8), members)
            ref[rows, :] = one_level(first + k)
            return carry

        lax.fori_loop(0, count, body, 0)
        first += count


def from_subgrid(pert_ref, level, values, weight_ref, side_ref, sum_ref, out_ref):
    members, points = values.shape
    ratio = out_ref.shape[0]
    tiles = members // 8
    side_ref[0] = pltpu.roll(values, 1, axis=1)
    side_ref[1] = values
    side_ref[2] = pltpu.roll(values, points - 1, axis=1)
    for lane_tile in range(points // LANES):
        lanes = pl.ds(lane_tile * LANES, LANES)
        near = [[side_ref[j, pl.ds(8 * t, 8), lanes] for t in range(tiles)] for j in range(3)]
        for r in range(ratio):
            total = [None] * 3
            for t in range(tiles):
                pert = pert_ref[level, pl.ds(r * members + 8 * t, 8), lanes]
                for j in range(3):
                    term = pert * near[j][t]
                    total[j] = term if total[j] is None else total[j] + term
            mixed = None
            for j in range(3):
                term = total[j] * weight_ref[j, lane_tile, pl.ds(r, 8, stride=0), :]
                mixed = term if mixed is None else mixed + term
            sum_ref[pl.ds(8 * r, 8), :] = mixed
        result = sum_ref[pl.ds(0, ratio, stride=8), :]
        for k in range(1, 8):
            result = result + sum_ref[pl.ds(k, ratio, stride=8), :]
        out_ref[:, lanes] = result


def split(x):
    hi = x.astype(jnp.bfloat16)
    return hi, (x - hi.astype(jnp.float32)).astype(jnp.bfloat16)


def band_product(pieces, hi_ref, lo_ref, out_ref):
    halves = [split(ref[...]) for ref in pieces]
    for block in range(out_ref.shape[1] // REACH):
        cols = pl.ds(block * REACH, REACH)
        total = None
        for k in range(block, block + 3):
            hi, lo = halves[k]
            rows = pl.ds(k * REACH, REACH)
            for left, right_ref in ((hi, hi_ref), (lo, hi_ref), (hi, lo_ref)):
                term = jnp.dot(left, right_ref[rows, cols], preferred_element_type=jnp.float32)
                total = term if total is None else total + term
        out_ref[:, cols] = total


def wide(x, points):
    return jnp.concatenate([x] * (points // LANES), axis=1)


def totals(dots_ref, count):
    total = jnp.sum(dots_ref[...], axis=0)
    return [total[k : k + 1] for k in range(count)]


def first_pair(dots_ref):
    rr, rw, ww, wn, nn = totals(dots_ref, 5)
    alpha0 = rr / rw
    gamma1 = rr - 2.0 * alpha0 * rw + alpha0 * alpha0 * ww
    beta1 = gamma1 / rr
    r1_w = rw - alpha0 * ww
    r1_w1 = rw - 2.0 * alpha0 * ww + alpha0 * alpha0 * wn
    w1_w = ww - alpha0 * wn
    w1_w1 = ww - 2.0 * alpha0 * wn + alpha0 * alpha0 * nn
    p1_s1 = r1_w1 + 2.0 * beta1 * r1_w + beta1 * beta1 * rw
    alpha1 = gamma1 / p1_s1
    r1_s1 = r1_w1 + beta1 * r1_w
    s1_s1 = w1_w1 + 2.0 * beta1 * w1_w + beta1 * beta1 * ww
    gamma2 = gamma1 - 2.0 * alpha1 * r1_s1 + alpha1 * alpha1 * s1_s1
    return alpha0, beta1, alpha1, gamma2 / gamma1


def last_pair(dots_ref):
    rr, rw, rs, ss, ws, zs, ps = totals(dots_ref, 7)
    alpha = rr / ps
    gamma = rr - 2.0 * alpha * rs + alpha * alpha * ss
    beta = gamma / rr
    r_w = rw - 2.0 * alpha * ws + alpha * alpha * zs
    p_s = r_w + 2.0 * beta * (rs - alpha * ss) + beta * beta * ps
    return alpha, beta, gamma / p_s


STATE_IN = {0: "r", 1: "rw", 2: "rwn", 3: "rwpsz"}
STATE_OUT = {0: "w", 1: "n", 2: "xrwpsz", 3: "z"}
NEXT = {0: "w", 1: "n", 2: "w"}


def apply_kernel(stage, parts, *refs):
    refs = list(refs)
    take = lambda n: [refs.pop(0) for _ in range(n)]
    pieces = take(4)
    hi_ref, lo_ref, pert_ref, weight_ref, error_ref = take(5)
    (scalar_in,) = take(1) if stage >= 2 else (None,)
    state = dict(zip(STATE_IN[stage], take(len(STATE_IN[stage]))))
    new = dict(zip(STATE_OUT[stage], take(len(STATE_OUT[stage]))))
    (scalar_out,) = take(1) if stage else (None,)
    part_refs = take(parts)
    conv_ref, side_ref, level_ref, sum_ref, image_ref = refs

    levels, ratio, points = error_ref.shape
    members = pert_ref.shape[1] // ratio
    band_product(pieces, hi_ref, lo_ref, conv_ref)

    if stage == 2:
        steps = first_pair(scalar_in)
        scalar_out[0:1] = steps[3]
        alpha0, beta1, alpha1, beta2 = [wide(x, points) for x in steps]
    if stage == 3:
        beta2 = wide(scalar_in[0:1], points)
    counts = {0: 0, 1: 5, 2: 0, 3: 7}[stage]

    def one_level(level, carry):
        rows = pl.ds(pl.multiple_of(level * members, 8), members)
        from_subgrid(pert_ref, level, conv_ref[rows, :], weight_ref, side_ref, sum_ref, image_ref)
        mean = image_ref[...] * (1.0 / (MEMBERS - 1))
        old = {name: ref[level] for name, ref in state.items()}
        if stage == 0:
            new["w"][level] = error_ref[level] * old["r"] + mean
            products = []
        elif stage == 1:
            r, w = old["r"], old["w"]
            n = error_ref[level] * w + mean
            new["n"][level] = n
            products = [r * r, r * w, w * w, w * n, n * n]
        elif stage == 2:
            r, w, n = old["r"], old["w"], old["n"]
            m = error_ref[level] * n + mean
            r1, w1, n1 = r - alpha0 * w, w - alpha0 * n, n - alpha0 * m
            p, s, z = r1 + beta1 * r, w1 + beta1 * w, n1 + beta1 * n
            new["x"][level] = alpha0 * r + alpha1 * p
            r, w = r1 - alpha1 * s, w1 - alpha1 * z
            new["r"][level] = r
            new["w"][level] = w
            new["p"][level] = r + beta2 * p
            new["s"][level] = w + beta2 * s
            new["z"][level] = z
            products = []
        else:
            r, w, p, s = (old[name] for name in "rwps")
            z = error_ref[level] * w + mean + beta2 * old["z"]
            new["z"][level] = z
            products = [r * r, r * w, r * s, s * s, w * s, z * s, p * s]
        return tuple(c + sum(x[k : k + 8] for k in range(0, ratio, 8)) for c, x in zip(carry, products))

    zero = jnp.zeros((8, points), jnp.float32)
    total = lax.fori_loop(0, levels, one_level, (zero,) * counts)
    if counts:
        rows = [jnp.broadcast_to(jnp.sum(t, keepdims=True), (1, LANES)) for t in total]
        rows += [jnp.zeros((8 - counts, LANES), jnp.float32)]
        scalar_out[...] = jnp.broadcast_to(jnp.concatenate(rows, axis=0)[None], scalar_out.shape)
    if parts:
        to_subgrid(pert_ref, new[NEXT[stage]], weight_ref, part_refs, level_ref, side_ref)


def final_kernel(dots_ref, x_ref, r_ref, w_ref, p_ref, s_ref, z_ref, x_out, r_out, stack_ref):
    levels, ratio, points = x_ref.shape
    alpha2, beta3, alpha3 = last_pair(dots_ref)
    matrices = permutations(transposed=True)
    rows = stack_ref.shape[1] // ratio
    stack_ref[...] = jnp.zeros_like(stack_ref)
    groups = []
    for group in range(points // LANES):
        lanes = pl.ds(group * LANES, LANES)
        for level in range(levels):
            r, w, p, s = (ref[level, :, lanes] for ref in (r_ref, w_ref, p_ref, s_ref))
            r3 = r - alpha2 * s
            w3 = w - alpha2 * z_ref[level, :, lanes]
            x = x_ref[level, :, lanes] + alpha2 * p + alpha3 * (r3 + beta3 * p)
            stack_ref[group, pl.ds(level * ratio, ratio), :] = x
            r4 = r3 - alpha3 * (w3 + beta3 * s)
            stack_ref[group, pl.ds((8 + level) * ratio, ratio), :] = r4
        groups.append(
            [three_terms(stack_ref[group, pl.ds(r, rows, stride=ratio), :]) for r in range(ratio)]
        )
    for group, tiles in enumerate(turn_back(groups, matrices)):
        for t, tile in enumerate(tiles):
            tile = sum_of_terms(tile)
            cols = pl.ds(group * GROUP + t * LANES, LANES)
            x_out[:, cols] = tile[:levels]
            r_out[:, cols] = tile[8 : 8 + levels]


def vertical_kernel(coupling_ref, below_ref, *refs):
    *own_refs, above_ref, left_ref, right_ref = refs
    where = []
    for ref in (below_ref, *own_refs, above_ref):
        for k in range(ref.shape[0] // MEMBERS):
            where.append((ref, k * MEMBERS))
    levels = len(where) - 4
    first = lax.axis_index("lev") * levels - 1
    all_levels = coupling_ref.shape[0]
    coupling = []
    for k in range(levels + 2):
        at = jnp.clip(first + k, 0, all_levels - 1)
        coupling.append(jnp.where(at == first + k, coupling_ref[at], 0.0))

    def body(t, carry):
        field = [ref[pl.ds(base + pl.multiple_of(t * 8, 8), 8), :] for ref, base in where]
        stepped = [
            field[l + 1] + coupling[l] * (field[l] + field[l + 2]) for l in range(levels + 2)
        ]
        scaled = [coupling[l] * stepped[l] for l in range(levels + 2)]
        for l in range(levels):
            value = stepped[l + 1] + (scaled[l] + scaled[l + 2])
            rows = pl.ds(l * MEMBERS + pl.multiple_of(t * 8, 8), 8)
            left_ref[rows, :] = value[:, :REACH]
            right_ref[rows, :] = value[:, value.shape[1] - REACH :]
        return carry

    lax.fori_loop(0, MEMBERS // 8, body, 0)


def permutations(transposed=False):
    row = lax.broadcasted_iota(jnp.int32, (PAIR, PAIR), 1 if transposed else 0)
    col = lax.broadcasted_iota(jnp.int32, (PAIR, PAIR), 0 if transposed else 1)
    targets = [(row % 16) * 16 + row // 16]
    for kept in (2, 1, 0):
        low = 6 - kept
        new, out = row // 128, (row // 64) % 2
        middle, rest = (row % 64) >> low, row % (1 << low)
        targets.append(out * 128 + (middle << (low + 1)) + (new << low) + rest)
    return [jnp.where(target == col, 1.0, 0.0).astype(jnp.bfloat16) for target in targets]


def reorder(tiles):
    return [tiles[sum(((r >> i) & 1) << (3 - i) for i in range(4))] for r in range(16)]


def permute_pairs(groups, bit, matrix):
    rows = groups[0][0].shape[0]
    pairs = [(g, k, k + bit) for g in range(len(groups)) for k in range(16) if not k & bit]
    stacked = [jnp.concatenate([groups[g][a], groups[g][b]], axis=1) for g, a, b in pairs]
    stacked = jnp.concatenate(stacked, axis=0).astype(jnp.bfloat16)
    turned = jnp.dot(stacked, matrix, preferred_element_type=jnp.float32)
    result = [[None] * 16 for _ in groups]
    for i, (g, *pair) in enumerate(pairs):
        for half, k in enumerate(pair):
            lanes = slice(half * LANES, (half + 1) * LANES)
            result[g][k] = turned[i * rows : (i + 1) * rows, lanes]
    return result


def turn(groups, matrices):
    for bit, matrix in zip((1, 2, 4, 8), matrices):
        groups = permute_pairs(groups, bit, matrix)
    return [reorder(tiles) for tiles in groups]


def turn_back(groups, matrices):
    groups = [reorder(tiles) for tiles in groups]
    for bit, matrix in reversed(list(zip((1, 2, 4, 8), matrices))):
        groups = permute_pairs(groups, bit, matrix)
    return groups


def three_terms(x):
    hi = x.astype(jnp.bfloat16).astype(jnp.float32)
    rest = x - hi
    middle = rest.astype(jnp.bfloat16).astype(jnp.float32)
    return jnp.concatenate([hi, middle, rest - middle], axis=0)


def sum_of_terms(x):
    rows = x.shape[0] // 3
    return x[:rows] + (x[rows : 2 * rows] + x[2 * rows :])


def start_kernel(
    parts, rhs_ref, error_ref, slot_ref, weight_ref, pert_ref, field_ref, error_out, weight_out, *refs
):
    pert_out, *refs = refs
    part_refs = refs[:parts]
    stack_ref, turn_ref, fetched_ref, level_ref, side_ref, sems = refs[parts:]
    levels, members, columns = pert_ref.shape
    ratio = RATIO
    copies = [
        pltpu.make_async_copy(pert_ref.at[l], fetched_ref.at[l], sems.at[l]) for l in range(levels)
    ]
    for copy in copies:
        copy.start()

    stack_ref[...] = jnp.zeros_like(stack_ref)
    stack_ref[0:levels] = rhs_ref[...]
    stack_ref[8 : 8 + levels] = error_ref[...]
    weight = weight_ref[...]
    column = lax.broadcasted_iota(jnp.int32, weight.shape, 1)
    is_lower = slot_ref[...] < column // ratio
    stack_ref[5:6] = jnp.where(is_lower, weight, 0.0)
    stack_ref[6:7] = jnp.where(is_lower, 1.0 - weight, weight)
    stack_ref[7:8] = jnp.where(is_lower, 0.0, 1.0 - weight)
    matrices = permutations()
    rows = stack_ref.shape[0]
    groups = [
        [three_terms(stack_ref[:, pl.ds(g * GROUP + t * LANES, LANES)]) for t in range(16)]
        for g in range(columns // GROUP)
    ]
    for group, tiles in enumerate(turn(groups, matrices)):
        for r, tile in enumerate(tiles):
            turn_ref[pl.ds(r * rows, rows), :] = sum_of_terms(tile)
        point = pl.ds(group * LANES, LANES)
        picked = lambda f: turn_ref[pl.ds(f, ratio, stride=rows), :]
        for level in range(levels):
            field_ref[level, :, point] = picked(level)
            error_out[level, :, point] = picked(8 + level)
        for j in range(3):
            weight_out[j, group] = picked(5 + j)

    for level in range(levels):
        copies[level].wait()

        groups = [
            [
                fetched_ref[level, :, pl.ds(g * GROUP + t * LANES, LANES)].astype(jnp.float32)
                for t in range(16)
            ]
            for g in range(columns // GROUP)
        ]
        for group, tiles in enumerate(turn(groups, matrices)):
            for r, tile in enumerate(tiles):
                at = pl.ds(r * members, members)
                pert_out[level, at, pl.ds(group * LANES, LANES)] = tile
    to_subgrid(pert_out, field_ref, weight_out, part_refs, level_ref, side_ref)


def whole():
    return pl.BlockSpec(memory_space=pltpu.VMEM)


def scalars():
    return pl.BlockSpec(memory_space=pltpu.SMEM)


def call(kernel, args, out_shape, scratch=(), flops=0, in_specs=None):
    size = sum(np.prod(a.shape) * a.dtype.itemsize for a in args)
    return pl.pallas_call(
        kernel,
        in_specs=in_specs or [whole()] * len(args),
        out_specs=jax.tree.map(lambda _: whole(), out_shape),
        out_shape=out_shape,
        scratch_shapes=list(scratch),
        compiler_params=pltpu.CompilerParams(vmem_limit_bytes=VMEM_LIMIT),
        cost_estimate=pl.CostEstimate(flops=flops, bytes_accessed=int(size), transcendentals=0),
    )(*args)


def f32(*shape):
    return jax.ShapeDtypeStruct(shape, jnp.float32)


def shift(block, axis, step, periodic):
    count = lax.axis_size(axis)
    pairs = [(i, (i + step) % count) for i in range(count) if periodic or 0 <= i + step < count]
    return lax.ppermute(block, axis, pairs)


def shards(
    increment_rhs,
    error_variance,
    perturbations,
    interp_slot,
    interp_weight,
    halo_rows,
    vertical_coupling,
):
    members, levels, columns = perturbations.shape
    points = columns // RATIO
    devices = lax.axis_size("patch") * lax.axis_size("lev")

    extended = points + 2 * REACH
    band_hi, band_lo = call(
        band_kernel,
        (halo_rows, jnp.asarray(block_products())),
        (jax.ShapeDtypeStruct((extended, points), jnp.bfloat16),) * 2,
        in_specs=[scalars(), whole()],
    )
    part_levels = (2, levels - 4, 2)
    part_shapes = tuple(f32(n * members, points) for n in part_levels)
    level_scratch = pltpu.VMEM((3, RATIO, LANES), jnp.float32)
    side_scratch = pltpu.VMEM((3, members, points), jnp.float32)
    grid_shape = f32(levels, RATIO, points)

    def extend(parts, dots):
        low, middle, high = parts
        from_below = shift(high, "lev", 1, False)
        from_above = shift(low, "lev", -1, False)
        half = f32(levels * members, REACH)
        left, right = call(
            vertical_kernel,
            (vertical_coupling, from_below, low, middle, high, from_above),
            (half, half),
            in_specs=[scalars()] + [whole()] * 5,
        )
        if dots is not None:
            dots, left, right = lax.optimization_barrier((dots, left, right))
        from_left = shift(right, "patch", 1, True)
        from_right = shift(left, "patch", -1, True)
        return (from_left, left, right, from_right), dots

    def reduce(dots):
        return lax.all_to_all(dots, ("patch", "lev"), 0, 0, tiled=True)

    def apply(stage, pieces, scalar, state):
        last = stage == ITERS - 1
        outs = [grid_shape] * len(STATE_OUT[stage])
        outs += {0: [], 2: [f32(8, LANES)]}.get(stage, [f32(devices, 8, LANES)])
        outs += [] if last else list(part_shapes)
        args = [*pieces, band_hi, band_lo, pert, weights, error]
        args += [scalar] if stage >= 2 else []
        args += [state[name] for name in STATE_IN[stage]]
        result = list(
            call(
                functools.partial(apply_kernel, stage, 0 if last else 3),
                args,
                tuple(outs),
                scratch=(
                    pltpu.VMEM((levels * members, points), jnp.float32),
                    side_scratch,
                    level_scratch,
                    pltpu.VMEM((8 * RATIO, LANES), jnp.float32),
                    pltpu.VMEM((RATIO, points), jnp.float32),
                ),
                flops=int(1e9),
            )
        )
        new = {name: result.pop(0) for name in STATE_OUT[stage]}
        return new, result.pop(0) if stage else None, result

    rhs, error, weights, pert, *parts = call(
        functools.partial(start_kernel, 3),
        (
            increment_rhs,
            error_variance,
            interp_slot[None],
            interp_weight[None],
            perturbations.transpose(1, 0, 2),
        ),
        (
            grid_shape,
            grid_shape,
            f32(3, points // LANES, RATIO, LANES),
            f32(levels, RATIO * members, points),
            *part_shapes,
        ),
        scratch=(
            pltpu.VMEM((16, columns), jnp.float32),
            pltpu.VMEM((16 * RATIO, LANES), jnp.float32),
            pltpu.VMEM((levels, members, columns), jnp.bfloat16),
            level_scratch,
            side_scratch,
            pltpu.SemaphoreType.DMA((levels,)),
        ),
        flops=int(1e8),
        in_specs=[whole()] * 4 + [pl.BlockSpec(memory_space=pltpu.HBM)],
    )
    state, scalar = dict(r=rhs), None
    for stage in range(ITERS):
        pieces, scalar = extend(parts, scalar)
        if stage == 2:
            scalar = reduce(scalar)
        new, scalar, parts = apply(stage, pieces, scalar, state)
        state.update(new)
    return call(
        final_kernel,
        (reduce(scalar), *(state[name] for name in "xrwpsz")),
        (f32(levels, columns),) * 2,
        scratch=(pltpu.VMEM((points // LANES, 16 * RATIO, LANES), jnp.float32),),
    )


def solution(mesh):
    in_specs = (
        P("lev", "patch"),
        P("lev", "patch"),
        P(None, "lev", "patch"),
        P("patch"),
        P("patch"),
        P(),
        P(),
    )
    out_specs = (P("lev", "patch"), P("lev", "patch"))
    return jax.shard_map(shards, mesh=mesh, in_specs=in_specs, out_specs=out_specs, check_vma=False)
```

```python
import functools

import jax
import jax.numpy as jnp
import numpy as np
from jax import lax
from jax.experimental import pallas as pl
from jax.experimental.pallas import tpu as pltpu
from jax.sharding import PartitionSpec as P

MEMBERS = 40
RATIO = 16
HALO = 128
ITERS = 4
LANES = 128
UNROLL = 8
REACH = 2 * HALO
VMEM_LIMIT = 24 * 1024 * 1024
GROUP = LANES * RATIO
PAIR = 2 * LANES


def tap_blocks():
    reach = np.arange(HALO + 1)
    rough = 0.5 + ((97 * reach * reach + 31 * reach) % 257) / 256.0
    raw = (1.0 - reach / (2.0 * HALO)) * rough
    taps = raw / np.sqrt(2.0 * np.sum(raw**2) - raw[0] ** 2)
    rows, cols = np.arange(HALO)[:, None], np.arange(HALO)[None, :]
    blocks = []
    for shift in range(3):
        distance = np.abs(rows - cols + (1 - shift) * HALO)
        blocks.append(np.where(distance <= HALO, taps[np.minimum(distance, HALO)], 0.0))
    return blocks


def block_products():
    blocks = tap_blocks()
    return np.stack([np.stack([a.T @ b for b in blocks]) for a in blocks]).astype(np.float32)


def band_kernel(halo_ref, prod_ref, hi_ref, lo_ref):
    patch, patches = lax.axis_index("patch"), lax.axis_size("patch")
    counts = [halo_ref[lax.rem(patch + patches + step, patches)] for step in (-1, 0, 1)]
    own_blocks = hi_ref.shape[1] // HALO
    edge = (0, own_blocks + 1)
    lane = lax.broadcasted_iota(jnp.int32, (HALO, HALO), 1)
    row = lax.broadcasted_iota(jnp.int32, (HALO, HALO), 0)
    crossing = {
        (0, 2): (counts[0], False),
        (1, 1): (counts[1], True),
        (own_blocks, own_blocks + 2): (counts[1], False),
        (own_blocks + 1, own_blocks + 1): (counts[2], True),
    }

    def keep(index, key):
        count, from_end = crossing[key]
        return (HALO - 1 - index if from_end else index) < count

    for source in range(own_blocks + 4):
        for target in range(2, own_blocks + 2):
            total = jnp.zeros((HALO, HALO), jnp.float32)
            for i in range(edge[0], edge[1] + 1):
                a, b = source - i, target - i
                if not (0 <= a < 3 and 0 <= b < 3):
                    continue
                term = prod_ref[a, b]
                if (i, source) in crossing:
                    term = jnp.where(keep(row, (i, source)), term, 0.0)
                if (i, target) in crossing:
                    term = jnp.where(keep(lane, (i, target)), term, 0.0)
                total = total + term
            hi = total.astype(jnp.bfloat16)
            at = (pl.ds(source * HALO, HALO), pl.ds((target - 2) * HALO, HALO))
            hi_ref[at] = hi
            lo_ref[at] = (total - hi.astype(jnp.float32)).astype(jnp.bfloat16)


def to_subgrid(pert_ref, field_ref, weight_ref, part_refs, level_ref, side_ref):
    levels, ratio, points = field_ref.shape
    members = pert_ref.shape[1] // ratio
    tiles = members // 8

    def one_level(level):
        for lane_tile in range(points // LANES):
            lanes = pl.ds(lane_tile * LANES, LANES)
            field = field_ref[level, :, lanes]
            for j in range(3):
                level_ref[j] = field * weight_ref[j, lane_tile]
            def some_r(step, total, lanes=lanes):
                total = list(total)
                count = UNROLL * members
                at = pl.ds(pl.multiple_of(step * count, 8), count)
                perts = pert_ref.at[level, at, lanes]
                scales = level_ref.at[:, pl.ds(pl.multiple_of(step * UNROLL, UNROLL), UNROLL), :]
                for k in range(UNROLL):
                    scale = [scales[j, pl.ds(k, 8, stride=0), :] for j in range(3)]
                    for t in range(tiles):
                        pert = perts[k * members + 8 * t : k * members + 8 * t + 8, :]
                        for j in range(3):
                            total[j * tiles + t] += pert * scale[j]
                return tuple(total)

            zero = jnp.zeros((8, LANES), jnp.float32)
            total = lax.fori_loop(0, ratio // UNROLL, some_r, (zero,) * (3 * tiles))
            total = [total[j * tiles : (j + 1) * tiles] for j in range(3)]
            for j in range(3):
                for t in range(tiles):
                    side_ref[j, pl.ds(8 * t, 8), lanes] = total[j][t]
        return (
            side_ref[1]
            + pltpu.roll(side_ref[0], points - 1, axis=1)
            + pltpu.roll(side_ref[2], 1, axis=1)
        )

    first = 0
    for ref in part_refs:
        count = ref.shape[0] // members

        def body(k, carry, ref=ref, first=first):
            rows = pl.ds(pl.multiple_of(k * members, 8), members)
            ref[rows, :] = one_level(first + k)
            return carry

        lax.fori_loop(0, count, body, 0)
        first += count


def from_subgrid(pert_ref, level, values, weight_ref, side_ref, sum_ref, out_ref):
    members, points = values.shape
    ratio = out_ref.shape[0]
    tiles = members // 8
    side_ref[0] = pltpu.roll(values, 1, axis=1)
    side_ref[1] = values
    side_ref[2] = pltpu.roll(values, points - 1, axis=1)
    for lane_tile in range(points // LANES):
        lanes = pl.ds(lane_tile * LANES, LANES)
        near = [[side_ref[j, pl.ds(8 * t, 8), lanes] for t in range(tiles)] for j in range(3)]
        def some_r(step, carry, lanes=lanes, near=near, lane_tile=lane_tile):
            count = UNROLL * members
            at = pl.ds(pl.multiple_of(step * count, 8), count)
            perts = pert_ref.at[level, at, lanes]
            some = pl.ds(pl.multiple_of(step * UNROLL, UNROLL), UNROLL)
            weights = weight_ref.at[:, lane_tile, some, :]
            count = 8 * UNROLL
            sum_at = sum_ref.at[pl.ds(pl.multiple_of(step * count, 8), count), :]
            for k in range(UNROLL):
                total = [None] * 3
                for t in range(tiles):
                    pert = perts[k * members + 8 * t : k * members + 8 * t + 8, :]
                    for j in range(3):
                        term = pert * near[j][t]
                        total[j] = term if total[j] is None else total[j] + term
                mixed = None
                for j in range(3):
                    term = total[j] * weights[j, pl.ds(k, 8, stride=0), :]
                    mixed = term if mixed is None else mixed + term
                sum_at[8 * k : 8 * k + 8, :] = mixed
            return carry

        lax.fori_loop(0, ratio // UNROLL, some_r, 0)
        result = sum_ref[pl.ds(0, ratio, stride=8), :]
        for k in range(1, 8):
            result = result + sum_ref[pl.ds(k, ratio, stride=8), :]
        out_ref[:, lanes] = result


def split(x):
    hi = x.astype(jnp.bfloat16)
    return hi, (x - hi.astype(jnp.float32)).astype(jnp.bfloat16)


def band_product(pieces, hi_ref, lo_ref, out_ref):
    halves = [split(ref[...]) for ref in pieces]
    for block in range(out_ref.shape[1] // REACH):
        cols = pl.ds(block * REACH, REACH)
        total = None
        for k in range(block, block + 3):
            hi, lo = halves[k]
            rows = pl.ds(k * REACH, REACH)
            for left, right_ref in ((hi, hi_ref), (lo, hi_ref), (hi, lo_ref)):
                term = jnp.dot(left, right_ref[rows, cols], preferred_element_type=jnp.float32)
                total = term if total is None else total + term
        out_ref[:, cols] = total


def wide(x, points):
    return jnp.concatenate([x] * (points // LANES), axis=1)


def totals(dots_ref, count):
    total = jnp.sum(dots_ref[...], axis=0)
    lane = lax.broadcasted_iota(jnp.int32, total.shape, 1)
    picked = [jnp.sum(jnp.where(lane == k, total, 0.0), keepdims=True) for k in range(count)]
    return [jnp.broadcast_to(x, total.shape) for x in picked]


def first_pair(dots_ref):
    rr, rw, ww, wn, nn = totals(dots_ref, 5)
    alpha0 = rr / rw
    gamma1 = rr - 2.0 * alpha0 * rw + alpha0 * alpha0 * ww
    beta1 = gamma1 / rr
    r1_w = rw - alpha0 * ww
    r1_w1 = rw - 2.0 * alpha0 * ww + alpha0 * alpha0 * wn
    w1_w = ww - alpha0 * wn
    w1_w1 = ww - 2.0 * alpha0 * wn + alpha0 * alpha0 * nn
    p1_s1 = r1_w1 + 2.0 * beta1 * r1_w + beta1 * beta1 * rw
    alpha1 = gamma1 / p1_s1
    r1_s1 = r1_w1 + beta1 * r1_w
    s1_s1 = w1_w1 + 2.0 * beta1 * w1_w + beta1 * beta1 * ww
    gamma2 = gamma1 - 2.0 * alpha1 * r1_s1 + alpha1 * alpha1 * s1_s1
    return alpha0, beta1, alpha1, gamma2 / gamma1


def last_pair(dots_ref):
    rr, rw, rs, ss, ws, zs, ps = totals(dots_ref, 7)
    alpha = rr / ps
    gamma = rr - 2.0 * alpha * rs + alpha * alpha * ss
    beta = gamma / rr
    r_w = rw - 2.0 * alpha * ws + alpha * alpha * zs
    p_s = r_w + 2.0 * beta * (rs - alpha * ss) + beta * beta * ps
    return alpha, beta, gamma / p_s


STATE_IN = {0: "r", 1: "rw", 2: "rwn", 3: "rwpsz"}
STATE_OUT = {0: "w", 1: "n", 2: "xrwpsz", 3: "z"}
NEXT = {0: "w", 1: "n", 2: "w"}


def apply_kernel(stage, parts, *refs):
    refs = list(refs)
    take = lambda n: [refs.pop(0) for _ in range(n)]
    pieces = take(4)
    hi_ref, lo_ref, pert_ref, weight_ref, error_ref = take(5)
    (scalar_in,) = take(1) if stage >= 2 else (None,)
    state = dict(zip(STATE_IN[stage], take(len(STATE_IN[stage]))))
    new = dict(zip(STATE_OUT[stage], take(len(STATE_OUT[stage]))))
    (scalar_out,) = take(1) if stage else (None,)
    part_refs = take(parts)
    conv_ref, side_ref, level_ref, sum_ref, image_ref = refs

    levels, ratio, points = error_ref.shape
    members = pert_ref.shape[1] // ratio
    band_product(pieces, hi_ref, lo_ref, conv_ref)

    if stage == 2:
        steps = first_pair(scalar_in)
        scalar_out[0:1] = steps[3]
        alpha0, beta1, alpha1, beta2 = [wide(x, points) for x in steps]
    if stage == 3:
        beta2 = wide(scalar_in[0:1], points)
    counts = {0: 0, 1: 5, 2: 0, 3: 7}[stage]

    def one_level(level, carry):
        rows = pl.ds(pl.multiple_of(level * members, 8), members)
        from_subgrid(pert_ref, level, conv_ref[rows, :], weight_ref, side_ref, sum_ref, image_ref)
        mean = image_ref[...] * (1.0 / (MEMBERS - 1))
        old = {name: ref[level] for name, ref in state.items()}
        if stage == 0:
            new["w"][level] = error_ref[level] * old["r"] + mean
            products = []
        elif stage == 1:
            r, w = old["r"], old["w"]
            n = error_ref[level] * w + mean
            new["n"][level] = n
            products = [r * r, r * w, w * w, w * n, n * n]
        elif stage == 2:
            r, w, n = old["r"], old["w"], old["n"]
            m = error_ref[level] * n + mean
            r1, w1, n1 = r - alpha0 * w, w - alpha0 * n, n - alpha0 * m
            p, s, z = r1 + beta1 * r, w1 + beta1 * w, n1 + beta1 * n
            new["x"][level] = alpha0 * r + alpha1 * p
            r, w = r1 - alpha1 * s, w1 - alpha1 * z
            new["r"][level] = r
            new["w"][level] = w
            new["p"][level] = r + beta2 * p
            new["s"][level] = w + beta2 * s
            new["z"][level] = z
            products = []
        else:
            r, w, p, s = (old[name] for name in "rwps")
            z = error_ref[level] * w + mean + beta2 * old["z"]
            new["z"][level] = z
            products = [r * r, r * w, r * s, s * s, w * s, z * s, p * s]
        return tuple(c + sum(x[k : k + 8] for k in range(0, ratio, 8)) for c, x in zip(carry, products))

    zero = jnp.zeros((8, points), jnp.float32)
    total = lax.fori_loop(0, levels, one_level, (zero,) * counts)
    if counts:
        lane = lax.broadcasted_iota(jnp.int32, (1, LANES), 1)
        row = jnp.zeros((1, LANES), jnp.float32)
        for k, t in enumerate(total):
            row = jnp.where(lane == k, jnp.sum(t, keepdims=True), row)
        scalar_out[...] = jnp.broadcast_to(row[None], scalar_out.shape)
    if parts:
        to_subgrid(pert_ref, new[NEXT[stage]], weight_ref, part_refs, level_ref, side_ref)


def final_kernel(dots_ref, x_ref, r_ref, w_ref, p_ref, s_ref, z_ref, x_out, r_out, stack_ref):
    levels, ratio, points = x_ref.shape
    alpha2, beta3, alpha3 = last_pair(dots_ref)
    matrices = permutations(transposed=True)
    rows = stack_ref.shape[1] // ratio
    stack_ref[...] = jnp.zeros_like(stack_ref)
    groups = []
    for group in range(points // LANES):
        lanes = pl.ds(group * LANES, LANES)
        for level in range(levels):
            r, w, p, s = (ref[level, :, lanes] for ref in (r_ref, w_ref, p_ref, s_ref))
            r3 = r - alpha2 * s
            w3 = w - alpha2 * z_ref[level, :, lanes]
            x = x_ref[level, :, lanes] + alpha2 * p + alpha3 * (r3 + beta3 * p)
            stack_ref[group, pl.ds(level * ratio, ratio), :] = x
            r4 = r3 - alpha3 * (w3 + beta3 * s)
            stack_ref[group, pl.ds((8 + level) * ratio, ratio), :] = r4
        groups.append(
            [three_terms(stack_ref[group, pl.ds(r, rows, stride=ratio), :]) for r in range(ratio)]
        )
    for group, tiles in enumerate(turn_back(groups, matrices)):
        for t, tile in enumerate(tiles):
            tile = sum_of_terms(tile)
            cols = pl.ds(group * GROUP + t * LANES, LANES)
            x_out[:, cols] = tile[:levels]
            r_out[:, cols] = tile[8 : 8 + levels]


def vertical_kernel(coupling_ref, below_ref, *refs):
    *own_refs, above_ref, left_ref, right_ref = refs
    where = []
    for ref in (below_ref, *own_refs, above_ref):
        for k in range(ref.shape[0] // MEMBERS):
            where.append((ref, k * MEMBERS))
    levels = len(where) - 4
    first = lax.axis_index("lev") * levels - 1
    all_levels = coupling_ref.shape[0]
    coupling = []
    for k in range(levels + 2):
        at = jnp.clip(first + k, 0, all_levels - 1)
        coupling.append(jnp.where(at == first + k, coupling_ref[at], 0.0))

    def body(t, carry):
        field = [ref[pl.ds(base + pl.multiple_of(t * 8, 8), 8), :] for ref, base in where]
        stepped = [
            field[l + 1] + coupling[l] * (field[l] + field[l + 2]) for l in range(levels + 2)
        ]
        scaled = [coupling[l] * stepped[l] for l in range(levels + 2)]
        for l in range(levels):
            value = stepped[l + 1] + (scaled[l] + scaled[l + 2])
            rows = pl.ds(l * MEMBERS + pl.multiple_of(t * 8, 8), 8)
            left_ref[rows, :] = value[:, :REACH]
            right_ref[rows, :] = value[:, value.shape[1] - REACH :]
        return carry

    lax.fori_loop(0, MEMBERS // 8, body, 0)


def permutations(transposed=False):
    row = lax.broadcasted_iota(jnp.int32, (PAIR, PAIR), 1 if transposed else 0)
    col = lax.broadcasted_iota(jnp.int32, (PAIR, PAIR), 0 if transposed else 1)
    targets = [(row % 16) * 16 + row // 16]
    for kept in (2, 1, 0):
        low = 6 - kept
        new, out = row // 128, (row // 64) % 2
        middle, rest = (row % 64) >> low, row % (1 << low)
        targets.append(out * 128 + (middle << (low + 1)) + (new << low) + rest)
    return [jnp.where(target == col, 1.0, 0.0).astype(jnp.bfloat16) for target in targets]


def reorder(tiles):
    return [tiles[sum(((r >> i) & 1) << (3 - i) for i in range(4))] for r in range(16)]


def permute_pairs(groups, bit, matrix):
    rows = groups[0][0].shape[0]
    pairs = [(g, k, k + bit) for g in range(len(groups)) for k in range(16) if not k & bit]
    stacked = [jnp.concatenate([groups[g][a], groups[g][b]], axis=1) for g, a, b in pairs]
    stacked = jnp.concatenate(stacked, axis=0).astype(jnp.bfloat16)
    turned = jnp.dot(stacked, matrix, preferred_element_type=jnp.float32)
    result = [[None] * 16 for _ in groups]
    for i, (g, *pair) in enumerate(pairs):
        for half, k in enumerate(pair):
            lanes = slice(half * LANES, (half + 1) * LANES)
            result[g][k] = turned[i * rows : (i + 1) * rows, lanes]
    return result


def turn(groups, matrices):
    for bit, matrix in zip((1, 2, 4, 8), matrices):
        groups = permute_pairs(groups, bit, matrix)
    return [reorder(tiles) for tiles in groups]


def turn_back(groups, matrices):
    groups = [reorder(tiles) for tiles in groups]
    for bit, matrix in reversed(list(zip((1, 2, 4, 8), matrices))):
        groups = permute_pairs(groups, bit, matrix)
    return groups


def three_terms(x):
    hi = x.astype(jnp.bfloat16).astype(jnp.float32)
    rest = x - hi
    middle = rest.astype(jnp.bfloat16).astype(jnp.float32)
    return jnp.concatenate([hi, middle, rest - middle], axis=0)


def sum_of_terms(x):
    rows = x.shape[0] // 3
    return x[:rows] + (x[rows : 2 * rows] + x[2 * rows :])


def turn_fields(stack_ref, turn_ref, matrices, take):
    rows, columns = stack_ref.shape
    groups = [
        [three_terms(stack_ref[:, pl.ds(g * GROUP + t * LANES, LANES)]) for t in range(RATIO)]
        for g in range(columns // GROUP)
    ]
    for group, tiles in enumerate(turn(groups, matrices)):
        for r, tile in enumerate(tiles):
            turn_ref[group, pl.ds(r * rows, rows), :] = sum_of_terms(tile)
        take(group, lambda f: turn_ref[group, pl.ds(f, RATIO, stride=rows), :])


def error_kernel(error_ref, error_out, stack_ref, turn_ref):
    levels = error_ref.shape[0]
    stack_ref[...] = jnp.zeros_like(stack_ref)
    stack_ref[0:levels] = error_ref[...]

    def take(group, picked):
        for level in range(levels):
            error_out[level, :, pl.ds(group * LANES, LANES)] = picked(level)

    turn_fields(stack_ref, turn_ref, permutations(), take)


def start_kernel(
    parts, rhs_ref, slot_ref, weight_ref, pert_ref, field_ref, weight_out, pert_out, *refs
):
    part_refs = refs[:parts]
    stack_ref, turn_ref, level_ref, side_ref = refs[parts:]
    levels, members, columns = pert_ref.shape

    stack_ref[0:levels] = rhs_ref[...]
    weight = weight_ref[...]
    column = lax.broadcasted_iota(jnp.int32, weight.shape, 1)
    is_lower = slot_ref[...] < column // RATIO
    stack_ref[levels : levels + 1] = jnp.where(is_lower, weight, 0.0)
    stack_ref[levels + 1 : levels + 2] = jnp.where(is_lower, 1.0 - weight, weight)
    stack_ref[levels + 2 : levels + 3] = jnp.where(is_lower, 0.0, 1.0 - weight)
    matrices = permutations()

    def take(group, picked):
        for level in range(levels):
            field_ref[level, :, pl.ds(group * LANES, LANES)] = picked(level)
        for j in range(3):
            weight_out[j, group] = picked(levels + j)

    turn_fields(stack_ref, turn_ref, matrices, take)

    for level in range(levels):
        groups = [
            [
                pert_ref[level, :, pl.ds(g * GROUP + t * LANES, LANES)].astype(jnp.float32)
                for t in range(16)
            ]
            for g in range(columns // GROUP)
        ]
        for group, tiles in enumerate(turn(groups, matrices)):
            for r, tile in enumerate(tiles):
                at = pl.ds(r * members, members)
                pert_out[level, at, pl.ds(group * LANES, LANES)] = tile
    to_subgrid(pert_out, field_ref, weight_out, part_refs, level_ref, side_ref)


def whole():
    return pl.BlockSpec(memory_space=pltpu.VMEM)


def scalars():
    return pl.BlockSpec(memory_space=pltpu.SMEM)


def call(kernel, args, out_shape, scratch=(), flops=0, in_specs=None):
    size = sum(np.prod(a.shape) * a.dtype.itemsize for a in args)
    return pl.pallas_call(
        kernel,
        in_specs=in_specs or [whole()] * len(args),
        out_specs=jax.tree.map(lambda _: whole(), out_shape),
        out_shape=out_shape,
        scratch_shapes=list(scratch),
        compiler_params=pltpu.CompilerParams(vmem_limit_bytes=VMEM_LIMIT),
        cost_estimate=pl.CostEstimate(flops=flops, bytes_accessed=int(size), transcendentals=0),
    )(*args)


def f32(*shape):
    return jax.ShapeDtypeStruct(shape, jnp.float32)


def shift(block, axis, step, periodic):
    count = lax.axis_size(axis)
    pairs = [(i, (i + step) % count) for i in range(count) if periodic or 0 <= i + step < count]
    return lax.ppermute(block, axis, pairs)


def shards(
    increment_rhs,
    error_variance,
    perturbations,
    interp_slot,
    interp_weight,
    halo_rows,
    vertical_coupling,
):
    members, levels, columns = perturbations.shape
    points = columns // RATIO
    devices = lax.axis_size("patch") * lax.axis_size("lev")

    extended = points + 2 * REACH
    band_hi, band_lo = call(
        band_kernel,
        (halo_rows, jnp.asarray(block_products())),
        (jax.ShapeDtypeStruct((extended, points), jnp.bfloat16),) * 2,
        in_specs=[scalars(), whole()],
    )
    part_levels = (2, levels - 4, 2)
    part_shapes = tuple(f32(n * members, points) for n in part_levels)
    level_scratch = pltpu.VMEM((3, RATIO, LANES), jnp.float32)
    side_scratch = pltpu.VMEM((3, members, points), jnp.float32)
    grid_shape = f32(levels, RATIO, points)

    def extend(parts, dots):
        low, middle, high = parts
        from_below = shift(high, "lev", 1, False)
        from_above = shift(low, "lev", -1, False)
        half = f32(levels * members, REACH)
        left, right = call(
            vertical_kernel,
            (vertical_coupling, from_below, low, middle, high, from_above),
            (half, half),
            in_specs=[scalars()] + [whole()] * 5,
        )
        if dots is not None:
            dots, left, right = lax.optimization_barrier((dots, left, right))
        from_left = shift(right, "patch", 1, True)
        from_right = shift(left, "patch", -1, True)
        return (from_left, left, right, from_right), dots

    def reduce(dots):
        return lax.all_to_all(dots, ("patch", "lev"), 0, 0, tiled=True)

    def apply(stage, pieces, scalar, state):
        last = stage == ITERS - 1
        outs = [grid_shape] * len(STATE_OUT[stage])
        outs += {0: [], 2: [f32(8, LANES)]}.get(stage, [f32(devices, 1, LANES)])
        outs += [] if last else list(part_shapes)
        args = [*pieces, band_hi, band_lo, pert, weights, error]
        args += [scalar] if stage >= 2 else []
        args += [state[name] for name in STATE_IN[stage]]
        result = list(
            call(
                functools.partial(apply_kernel, stage, 0 if last else 3),
                args,
                tuple(outs),
                scratch=(
                    pltpu.VMEM((levels * members, points), jnp.float32),
                    side_scratch,
                    level_scratch,
                    pltpu.VMEM((8 * RATIO, LANES), jnp.float32),
                    pltpu.VMEM((RATIO, points), jnp.float32),
                ),
                flops=int(1e9),
            )
        )
        new = {name: result.pop(0) for name in STATE_OUT[stage]}
        return new, result.pop(0) if stage else None, result

    field_rows = 8 * pl.cdiv(levels + 3, 8)
    field_scratch = (
        pltpu.VMEM((field_rows, columns), jnp.float32),
        pltpu.VMEM((points // LANES, field_rows * RATIO, LANES), jnp.float32),
    )
    rhs, weights, pert, *parts = call(
        functools.partial(start_kernel, 3),
        (
            increment_rhs,
            interp_slot[None],
            interp_weight[None],
            perturbations.transpose(1, 0, 2),
        ),
        (
            grid_shape,
            f32(3, points // LANES, RATIO, LANES),
            f32(levels, RATIO * members, points),
            *part_shapes,
        ),
        scratch=(
            *field_scratch,
            level_scratch,
            side_scratch,
        ),
        flops=int(1e8),
    )
    error = call(error_kernel, (error_variance,), grid_shape, scratch=field_scratch, flops=int(1e7))
    state, scalar = dict(r=rhs), None
    for stage in range(ITERS):
        pieces, scalar = extend(parts, scalar)
        if stage == 2:
            scalar = reduce(scalar)
        new, scalar, parts = apply(stage, pieces, scalar, state)
        state.update(new)
    return call(
        final_kernel,
        (reduce(scalar), *(state[name] for name in "xrwpsz")),
        (f32(levels, columns),) * 2,
        scratch=(pltpu.VMEM((points // LANES, 16 * RATIO, LANES), jnp.float32),),
    )


def solution(mesh):
    in_specs = (
        P("lev", "patch"),
        P("lev", "patch"),
        P(None, "lev", "patch"),
        P("patch"),
        P("patch"),
        P(),
        P(),
    )
    out_specs = (P("lev", "patch"), P("lev", "patch"))
    return jax.shard_map(shards, mesh=mesh, in_specs=in_specs, out_specs=out_specs, check_vma=False)
```

```python
import functools

import jax
import jax.numpy as jnp
import numpy as np
from jax import lax
from jax.experimental import pallas as pl
from jax.experimental.pallas import tpu as pltpu
from jax.sharding import PartitionSpec as P

MEMBERS = 40
RATIO = 16
HALO = 128
ITERS = 4
LANES = 128
UNROLL = 8
REACH = 2 * HALO
VMEM_LIMIT = 24 * 1024 * 1024
GROUP = LANES * RATIO
PAIR = 2 * LANES


def tap_blocks():
    reach = np.arange(HALO + 1)
    rough = 0.5 + ((97 * reach * reach + 31 * reach) % 257) / 256.0
    raw = (1.0 - reach / (2.0 * HALO)) * rough
    taps = raw / np.sqrt(2.0 * np.sum(raw**2) - raw[0] ** 2)
    rows, cols = np.arange(HALO)[:, None], np.arange(HALO)[None, :]
    blocks = []
    for shift in range(3):
        distance = np.abs(rows - cols + (1 - shift) * HALO)
        blocks.append(np.where(distance <= HALO, taps[np.minimum(distance, HALO)], 0.0))
    return blocks


def block_products():
    blocks = tap_blocks()
    return np.stack([np.stack([a.T @ b for b in blocks]) for a in blocks]).astype(np.float32)


def band_kernel(levels, halo_ref, coupling_ref, prod_ref, hi_ref, lo_ref, coupling_out):
    first = lax.axis_index("lev") * levels - 1
    all_levels = coupling_ref.shape[0]
    coupling_out[...] = jnp.zeros_like(coupling_out)
    for k in range(levels + 2):
        at = jnp.clip(first + k, 0, all_levels - 1)
        value = jnp.where(at == first + k, coupling_ref[at], 0.0)
        coupling_out[pl.ds(k, 1), :] = jnp.full((1, LANES), value, jnp.float32)

    patch, patches = lax.axis_index("patch"), lax.axis_size("patch")
    counts = [halo_ref[lax.rem(patch + patches + step, patches)] for step in (-1, 0, 1)]
    own_blocks = hi_ref.shape[1] // HALO
    edge = (0, own_blocks + 1)
    lane = lax.broadcasted_iota(jnp.int32, (HALO, HALO), 1)
    row = lax.broadcasted_iota(jnp.int32, (HALO, HALO), 0)
    crossing = {
        (0, 2): (counts[0], False),
        (1, 1): (counts[1], True),
        (own_blocks, own_blocks + 2): (counts[1], False),
        (own_blocks + 1, own_blocks + 1): (counts[2], True),
    }

    def keep(index, key):
        count, from_end = crossing[key]
        return (HALO - 1 - index if from_end else index) < count

    for source in range(own_blocks + 4):
        for target in range(2, own_blocks + 2):
            total = jnp.zeros((HALO, HALO), jnp.float32)
            for i in range(edge[0], edge[1] + 1):
                a, b = source - i, target - i
                if not (0 <= a < 3 and 0 <= b < 3):
                    continue
                term = prod_ref[a, b]
                if (i, source) in crossing:
                    term = jnp.where(keep(row, (i, source)), term, 0.0)
                if (i, target) in crossing:
                    term = jnp.where(keep(lane, (i, target)), term, 0.0)
                total = total + term
            hi = total.astype(jnp.bfloat16)
            at = (pl.ds(source * HALO, HALO), pl.ds((target - 2) * HALO, HALO))
            hi_ref[at] = hi
            lo_ref[at] = (total - hi.astype(jnp.float32)).astype(jnp.bfloat16)


def to_subgrid(pert_ref, field_ref, weight_ref, part_refs, level_ref, side_ref):
    levels, ratio, points = field_ref.shape
    members = pert_ref.shape[1] // ratio
    tiles = members // 8

    def one_level(level):
        for lane_tile in range(points // LANES):
            lanes = pl.ds(lane_tile * LANES, LANES)
            field = field_ref[level, :, lanes]
            for j in range(3):
                level_ref[j] = field * weight_ref[j, lane_tile]
            def some_r(step, total, lanes=lanes):
                total = list(total)
                count = UNROLL * members
                at = pl.ds(pl.multiple_of(step * count, 8), count)
                perts = pert_ref.at[level, at, lanes]
                scales = level_ref.at[:, pl.ds(pl.multiple_of(step * UNROLL, UNROLL), UNROLL), :]
                for k in range(UNROLL):
                    scale = [scales[j, pl.ds(k, 8, stride=0), :] for j in range(3)]
                    for t in range(tiles):
                        pert = perts[k * members + 8 * t : k * members + 8 * t + 8, :]
                        for j in range(3):
                            total[j * tiles + t] += pert * scale[j]
                return tuple(total)

            zero = jnp.zeros((8, LANES), jnp.float32)
            total = lax.fori_loop(0, ratio // UNROLL, some_r, (zero,) * (3 * tiles))
            total = [total[j * tiles : (j + 1) * tiles] for j in range(3)]
            for j in range(3):
                for t in range(tiles):
                    side_ref[j, pl.ds(8 * t, 8), lanes] = total[j][t]
        return (
            side_ref[1]
            + pltpu.roll(side_ref[0], points - 1, axis=1)
            + pltpu.roll(side_ref[2], 1, axis=1)
        )

    first = 0
    for ref in part_refs:
        count = ref.shape[0] // members

        def body(k, carry, ref=ref, first=first):
            rows = pl.ds(pl.multiple_of(k * members, 8), members)
            ref[rows, :] = one_level(first + k)
            return carry

        lax.fori_loop(0, count, body, 0)
        first += count


def from_subgrid(pert_ref, level, values, weight_ref, side_ref, sum_ref, out_ref):
    members, points = values.shape
    ratio = out_ref.shape[0]
    tiles = members // 8
    side_ref[0] = pltpu.roll(values, 1, axis=1)
    side_ref[1] = values
    side_ref[2] = pltpu.roll(values, points - 1, axis=1)
    for lane_tile in range(points // LANES):
        lanes = pl.ds(lane_tile * LANES, LANES)
        near = [[side_ref[j, pl.ds(8 * t, 8), lanes] for t in range(tiles)] for j in range(3)]
        def some_r(step, carry, lanes=lanes, near=near, lane_tile=lane_tile):
            count = UNROLL * members
            at = pl.ds(pl.multiple_of(step * count, 8), count)
            perts = pert_ref.at[level, at, lanes]
            some = pl.ds(pl.multiple_of(step * UNROLL, UNROLL), UNROLL)
            weights = weight_ref.at[:, lane_tile, some, :]
            count = 8 * UNROLL
            sum_at = sum_ref.at[pl.ds(pl.multiple_of(step * count, 8), count), :]
            for k in range(UNROLL):
                total = [None] * 3
                for t in range(tiles):
                    pert = perts[k * members + 8 * t : k * members + 8 * t + 8, :]
                    for j in range(3):
                        term = pert * near[j][t]
                        total[j] = term if total[j] is None else total[j] + term
                mixed = None
                for j in range(3):
                    term = total[j] * weights[j, pl.ds(k, 8, stride=0), :]
                    mixed = term if mixed is None else mixed + term
                sum_at[8 * k : 8 * k + 8, :] = mixed
            return carry

        lax.fori_loop(0, ratio // UNROLL, some_r, 0)
        result = sum_ref[pl.ds(0, ratio, stride=8), :]
        for k in range(1, 8):
            result = result + sum_ref[pl.ds(k, ratio, stride=8), :]
        out_ref[:, lanes] = result


def split(x):
    hi = x.astype(jnp.bfloat16)
    return hi, (x - hi.astype(jnp.float32)).astype(jnp.bfloat16)


def band_product(pieces, hi_ref, lo_ref, out_ref):
    halves = [split(ref[...]) for ref in pieces]
    for block in range(out_ref.shape[1] // REACH):
        cols = pl.ds(block * REACH, REACH)
        total = None
        for k in range(block, block + 3):
            hi, lo = halves[k]
            rows = pl.ds(k * REACH, REACH)
            for left, right_ref in ((hi, hi_ref), (lo, hi_ref), (hi, lo_ref)):
                term = jnp.dot(left, right_ref[rows, cols], preferred_element_type=jnp.float32)
                total = term if total is None else total + term
        out_ref[:, cols] = total


def wide(x, points):
    return jnp.concatenate([x] * (points // LANES), axis=1)


def totals(dots_ref, count):
    total = jnp.sum(dots_ref[...], axis=0)
    lane = lax.broadcasted_iota(jnp.int32, total.shape, 1)
    picked = [jnp.sum(jnp.where(lane == k, total, 0.0), keepdims=True) for k in range(count)]
    return [jnp.broadcast_to(x, total.shape) for x in picked]


def first_pair(dots_ref):
    rr, rw, ww, wn, nn = totals(dots_ref, 5)
    alpha0 = rr / rw
    gamma1 = rr - 2.0 * alpha0 * rw + alpha0 * alpha0 * ww
    beta1 = gamma1 / rr
    r1_w = rw - alpha0 * ww
    r1_w1 = rw - 2.0 * alpha0 * ww + alpha0 * alpha0 * wn
    w1_w = ww - alpha0 * wn
    w1_w1 = ww - 2.0 * alpha0 * wn + alpha0 * alpha0 * nn
    p1_s1 = r1_w1 + 2.0 * beta1 * r1_w + beta1 * beta1 * rw
    alpha1 = gamma1 / p1_s1
    r1_s1 = r1_w1 + beta1 * r1_w
    s1_s1 = w1_w1 + 2.0 * beta1 * w1_w + beta1 * beta1 * ww
    gamma2 = gamma1 - 2.0 * alpha1 * r1_s1 + alpha1 * alpha1 * s1_s1
    return alpha0, beta1, alpha1, gamma2 / gamma1


def last_pair(dots_ref):
    rr, rw, rs, ss, ws, zs, ps = totals(dots_ref, 7)
    alpha = rr / ps
    gamma = rr - 2.0 * alpha * rs + alpha * alpha * ss
    beta = gamma / rr
    r_w = rw - 2.0 * alpha * ws + alpha * alpha * zs
    p_s = r_w + 2.0 * beta * (rs - alpha * ss) + beta * beta * ps
    return alpha, beta, gamma / p_s


STATE_IN = {0: "r", 1: "rw", 2: "rwn", 3: "rwpsz"}
STATE_OUT = {0: "w", 1: "n", 2: "xrwpsz", 3: "z"}
NEXT = {0: "w", 1: "n", 2: "w"}


def apply_kernel(stage, parts, *refs):
    refs = list(refs)
    take = lambda n: [refs.pop(0) for _ in range(n)]
    pieces = take(4)
    hi_ref, lo_ref, pert_ref, weight_ref, error_ref = take(5)
    (scalar_in,) = take(1) if stage >= 2 else (None,)
    state = dict(zip(STATE_IN[stage], take(len(STATE_IN[stage]))))
    new = dict(zip(STATE_OUT[stage], take(len(STATE_OUT[stage]))))
    (scalar_out,) = take(1) if stage else (None,)
    part_refs = take(parts)
    conv_ref, side_ref, level_ref, sum_ref, image_ref = refs

    levels, ratio, points = error_ref.shape
    members = pert_ref.shape[1] // ratio
    band_product(pieces, hi_ref, lo_ref, conv_ref)

    if stage == 2:
        steps = first_pair(scalar_in)
        scalar_out[0:1] = steps[3]
        alpha0, beta1, alpha1, beta2 = [wide(x, points) for x in steps]
    if stage == 3:
        beta2 = wide(scalar_in[0:1], points)
    counts = {0: 0, 1: 5, 2: 0, 3: 7}[stage]

    def one_level(level, carry):
        rows = pl.ds(pl.multiple_of(level * members, 8), members)
        from_subgrid(pert_ref, level, conv_ref[rows, :], weight_ref, side_ref, sum_ref, image_ref)
        mean = image_ref[...] * (1.0 / (MEMBERS - 1))
        old = {name: ref[level] for name, ref in state.items()}
        if stage == 0:
            new["w"][level] = error_ref[level] * old["r"] + mean
            products = []
        elif stage == 1:
            r, w = old["r"], old["w"]
            n = error_ref[level] * w + mean
            new["n"][level] = n
            products = [r * r, r * w, w * w, w * n, n * n]
        elif stage == 2:
            r, w, n = old["r"], old["w"], old["n"]
            m = error_ref[level] * n + mean
            r1, w1, n1 = r - alpha0 * w, w - alpha0 * n, n - alpha0 * m
            p, s, z = r1 + beta1 * r, w1 + beta1 * w, n1 + beta1 * n
            new["x"][level] = alpha0 * r + alpha1 * p
            r, w = r1 - alpha1 * s, w1 - alpha1 * z
            new["r"][level] = r
            new["w"][level] = w
            new["p"][level] = r + beta2 * p
            new["s"][level] = w + beta2 * s
            new["z"][level] = z
            products = []
        else:
            r, w, p, s = (old[name] for name in "rwps")
            z = error_ref[level] * w + mean + beta2 * old["z"]
            new["z"][level] = z
            products = [r * r, r * w, r * s, s * s, w * s, z * s, p * s]
        return tuple(c + sum(x[k : k + 8] for k in range(0, ratio, 8)) for c, x in zip(carry, products))

    zero = jnp.zeros((8, points), jnp.float32)
    total = lax.fori_loop(0, levels, one_level, (zero,) * counts)
    if counts:
        lane = lax.broadcasted_iota(jnp.int32, (1, LANES), 1)
        row = jnp.zeros((1, LANES), jnp.float32)
        for k, t in enumerate(total):
            row = jnp.where(lane == k, jnp.sum(t, keepdims=True), row)
        scalar_out[...] = jnp.broadcast_to(row[None], scalar_out.shape)
    if parts:
        to_subgrid(pert_ref, new[NEXT[stage]], weight_ref, part_refs, level_ref, side_ref)


def final_kernel(dots_ref, x_ref, r_ref, w_ref, p_ref, s_ref, z_ref, x_out, r_out, stack_ref):
    levels, ratio, points = x_ref.shape
    alpha2, beta3, alpha3 = last_pair(dots_ref)
    matrices = permutations(transposed=True)
    rows = stack_ref.shape[1] // ratio
    stack_ref[...] = jnp.zeros_like(stack_ref)
    groups = []
    for group in range(points // LANES):
        lanes = pl.ds(group * LANES, LANES)
        for level in range(levels):
            r, w, p, s = (ref[level, :, lanes] for ref in (r_ref, w_ref, p_ref, s_ref))
            r3 = r - alpha2 * s
            w3 = w - alpha2 * z_ref[level, :, lanes]
            x = x_ref[level, :, lanes] + alpha2 * p + alpha3 * (r3 + beta3 * p)
            stack_ref[group, pl.ds(level * ratio, ratio), :] = x
            r4 = r3 - alpha3 * (w3 + beta3 * s)
            stack_ref[group, pl.ds((8 + level) * ratio, ratio), :] = r4
        groups.append(
            [two_terms(stack_ref[group, pl.ds(r, rows, stride=ratio), :]) for r in range(ratio)]
        )
    for group, tiles in enumerate(turn_back(groups, matrices)):
        for t, tile in enumerate(tiles):
            tile = sum_of_terms(tile)
            cols = pl.ds(group * GROUP + t * LANES, LANES)
            x_out[:, cols] = tile[:levels]
            r_out[:, cols] = tile[8 : 8 + levels]


def vertical_kernel(coupling_ref, below_ref, *refs):
    *own_refs, above_ref, left_ref, right_ref = refs
    points = below_ref.shape[1]
    where = []
    for ref in (below_ref, *own_refs, above_ref):
        for k in range(ref.shape[0] // MEMBERS):
            where.append((ref, k * MEMBERS))
    levels = len(where) - 4
    coupling = [wide(coupling_ref[pl.ds(k, 8, stride=0), :], points) for k in range(levels + 2)]

    def body(t, carry):
        field = [ref[pl.ds(base + pl.multiple_of(t * 8, 8), 8), :] for ref, base in where]
        stepped = [
            field[l + 1] + coupling[l] * (field[l] + field[l + 2]) for l in range(levels + 2)
        ]
        scaled = [coupling[l] * stepped[l] for l in range(levels + 2)]
        for l in range(levels):
            value = stepped[l + 1] + (scaled[l] + scaled[l + 2])
            rows = pl.ds(l * MEMBERS + pl.multiple_of(t * 8, 8), 8)
            left_ref[rows, :] = value[:, :REACH]
            right_ref[rows, :] = value[:, points - REACH :]
        return carry

    lax.fori_loop(0, MEMBERS // 8, body, 0)


def permutations(transposed=False):
    row = lax.broadcasted_iota(jnp.int32, (PAIR, PAIR), 1 if transposed else 0)
    col = lax.broadcasted_iota(jnp.int32, (PAIR, PAIR), 0 if transposed else 1)
    targets = [(row % 16) * 16 + row // 16]
    for kept in (2, 1, 0):
        low = 6 - kept
        new, out = row // 128, (row // 64) % 2
        middle, rest = (row % 64) >> low, row % (1 << low)
        targets.append(out * 128 + (middle << (low + 1)) + (new << low) + rest)
    return [jnp.where(target == col, 1.0, 0.0).astype(jnp.bfloat16) for target in targets]


def reorder(tiles):
    return [tiles[sum(((r >> i) & 1) << (3 - i) for i in range(4))] for r in range(16)]


def permute_pairs(groups, bit, matrix):
    rows = groups[0][0].shape[0]
    pairs = [(g, k, k + bit) for g in range(len(groups)) for k in range(16) if not k & bit]
    stacked = [jnp.concatenate([groups[g][a], groups[g][b]], axis=1) for g, a, b in pairs]
    stacked = jnp.concatenate(stacked, axis=0).astype(jnp.bfloat16)
    turned = jnp.dot(stacked, matrix, preferred_element_type=jnp.float32)
    result = [[None] * 16 for _ in groups]
    for i, (g, *pair) in enumerate(pairs):
        for half, k in enumerate(pair):
            lanes = slice(half * LANES, (half + 1) * LANES)
            result[g][k] = turned[i * rows : (i + 1) * rows, lanes]
    return result


def turn(groups, matrices):
    for bit, matrix in zip((1, 2, 4, 8), matrices):
        groups = permute_pairs(groups, bit, matrix)
    return [reorder(tiles) for tiles in groups]


def turn_back(groups, matrices):
    groups = [reorder(tiles) for tiles in groups]
    for bit, matrix in reversed(list(zip((1, 2, 4, 8), matrices))):
        groups = permute_pairs(groups, bit, matrix)
    return groups


def two_terms(x):
    hi = x.astype(jnp.bfloat16).astype(jnp.float32)
    return jnp.concatenate([hi, x - hi], axis=0)


def sum_of_terms(x):
    rows = x.shape[0] // 2
    return x[:rows] + x[rows:]


def turn_fields(stack_ref, turn_ref, matrices, take):
    rows, columns = stack_ref.shape
    groups = [
        [two_terms(stack_ref[:, pl.ds(g * GROUP + t * LANES, LANES)]) for t in range(RATIO)]
        for g in range(columns // GROUP)
    ]
    for group, tiles in enumerate(turn(groups, matrices)):
        for r, tile in enumerate(tiles):
            turn_ref[group, pl.ds(r * rows, rows), :] = sum_of_terms(tile)
        take(group, lambda f: turn_ref[group, pl.ds(f, RATIO, stride=rows), :])


def error_kernel(error_ref, error_out, stack_ref, turn_ref):
    levels = error_ref.shape[0]
    stack_ref[...] = jnp.zeros_like(stack_ref)
    stack_ref[0:levels] = error_ref[...]

    def take(group, picked):
        for level in range(levels):
            error_out[level, :, pl.ds(group * LANES, LANES)] = picked(level)

    turn_fields(stack_ref, turn_ref, permutations(), take)


def start_kernel(
    parts,
    rhs_ref,
    slot_ref,
    weight_ref,
    pert_ref,
    field_ref,
    weight_out,
    pert_out,
    *refs,
):
    part_refs = refs[:parts]
    stack_ref, turn_ref, level_ref, side_ref = refs[parts:]
    levels, members, columns = pert_ref.shape

    stack_ref[0:levels] = rhs_ref[...]
    weight = weight_ref[...]
    column = lax.broadcasted_iota(jnp.int32, weight.shape, 1)
    is_lower = slot_ref[...] < column // RATIO
    stack_ref[levels : levels + 1] = jnp.where(is_lower, weight, 0.0)
    stack_ref[levels + 1 : levels + 2] = jnp.where(is_lower, 1.0 - weight, weight)
    stack_ref[levels + 2 : levels + 3] = jnp.where(is_lower, 0.0, 1.0 - weight)
    matrices = permutations()

    def take(group, picked):
        for level in range(levels):
            field_ref[level, :, pl.ds(group * LANES, LANES)] = picked(level)
        for j in range(3):
            weight_out[j, group] = picked(levels + j)

    turn_fields(stack_ref, turn_ref, matrices, take)

    for level in range(levels):
        groups = [
            [
                pert_ref[level, :, pl.ds(g * GROUP + t * LANES, LANES)].astype(jnp.float32)
                for t in range(16)
            ]
            for g in range(columns // GROUP)
        ]
        for group, tiles in enumerate(turn(groups, matrices)):
            for r, tile in enumerate(tiles):
                at = pl.ds(r * members, members)
                pert_out[level, at, pl.ds(group * LANES, LANES)] = tile
    to_subgrid(pert_out, field_ref, weight_out, part_refs, level_ref, side_ref)


def whole():
    return pl.BlockSpec(memory_space=pltpu.VMEM)


def scalars():
    return pl.BlockSpec(memory_space=pltpu.SMEM)


def call(kernel, args, out_shape, scratch=(), flops=0, in_specs=None):
    size = sum(np.prod(a.shape) * a.dtype.itemsize for a in args)
    return pl.pallas_call(
        kernel,
        in_specs=in_specs or [whole()] * len(args),
        out_specs=jax.tree.map(lambda _: whole(), out_shape),
        out_shape=out_shape,
        scratch_shapes=list(scratch),
        compiler_params=pltpu.CompilerParams(vmem_limit_bytes=VMEM_LIMIT),
        cost_estimate=pl.CostEstimate(flops=flops, bytes_accessed=int(size), transcendentals=0),
    )(*args)


def f32(*shape):
    return jax.ShapeDtypeStruct(shape, jnp.float32)


def shift(block, axis, step, periodic):
    count = lax.axis_size(axis)
    pairs = [(i, (i + step) % count) for i in range(count) if periodic or 0 <= i + step < count]
    return lax.ppermute(block, axis, pairs)


def shards(
    increment_rhs,
    error_variance,
    perturbations,
    interp_slot,
    interp_weight,
    halo_rows,
    vertical_coupling,
):
    members, levels, columns = perturbations.shape
    points = columns // RATIO
    devices = lax.axis_size("patch") * lax.axis_size("lev")

    extended = points + 2 * REACH
    band_hi, band_lo, couplings = call(
        functools.partial(band_kernel, levels),
        (halo_rows, vertical_coupling, jnp.asarray(block_products())),
        (
            jax.ShapeDtypeStruct((extended, points), jnp.bfloat16),
            jax.ShapeDtypeStruct((extended, points), jnp.bfloat16),
            f32(8 * pl.cdiv(levels + 2, 8), LANES),
        ),
        in_specs=[scalars(), scalars(), whole()],
    )
    part_levels = (2, levels - 4, 2)
    part_shapes = tuple(f32(n * members, points) for n in part_levels)
    level_scratch = pltpu.VMEM((3, RATIO, LANES), jnp.float32)
    side_scratch = pltpu.VMEM((3, members, points), jnp.float32)
    grid_shape = f32(levels, RATIO, points)

    def extend(parts, dots):
        low, middle, high = parts
        from_below = shift(high, "lev", 1, False)
        from_above = shift(low, "lev", -1, False)
        half = f32(levels * members, REACH)
        left, right = call(
            vertical_kernel,
            (couplings, from_below, low, middle, high, from_above),
            (half, half),
        )
        if dots is not None:
            dots, left, right = lax.optimization_barrier((dots, left, right))
        from_left = shift(right, "patch", 1, True)
        from_right = shift(left, "patch", -1, True)
        return (from_left, left, right, from_right), dots

    def reduce(dots):
        return lax.all_to_all(dots, ("patch", "lev"), 0, 0, tiled=True)

    def apply(stage, pieces, scalar, state):
        last = stage == ITERS - 1
        outs = [grid_shape] * len(STATE_OUT[stage])
        outs += {0: [], 2: [f32(8, LANES)]}.get(stage, [f32(devices, 1, LANES)])
        outs += [] if last else list(part_shapes)
        args = [*pieces, band_hi, band_lo, pert, weights, error]
        args += [scalar] if stage >= 2 else []
        args += [state[name] for name in STATE_IN[stage]]
        result = list(
            call(
                functools.partial(apply_kernel, stage, 0 if last else 3),
                args,
                tuple(outs),
                scratch=(
                    pltpu.VMEM((levels * members, points), jnp.float32),
                    side_scratch,
                    level_scratch,
                    pltpu.VMEM((8 * RATIO, LANES), jnp.float32),
                    pltpu.VMEM((RATIO, points), jnp.float32),
                ),
                flops=int(1e9),
            )
        )
        new = {name: result.pop(0) for name in STATE_OUT[stage]}
        return new, result.pop(0) if stage else None, result

    field_rows = 8 * pl.cdiv(levels + 3, 8)
    field_scratch = (
        pltpu.VMEM((field_rows, columns), jnp.float32),
        pltpu.VMEM((points // LANES, field_rows * RATIO, LANES), jnp.float32),
    )
    rhs, weights, pert, *parts = call(
        functools.partial(start_kernel, 3),
        (
            increment_rhs,
            interp_slot[None],
            interp_weight[None],
            perturbations.transpose(1, 0, 2),
        ),
        (
            grid_shape,
            f32(3, points // LANES, RATIO, LANES),
            f32(levels, RATIO * members, points),
            *part_shapes,
        ),
        scratch=(
            *field_scratch,
            level_scratch,
            side_scratch,
        ),
        flops=int(1e8),
    )
    error = call(error_kernel, (error_variance,), grid_shape, scratch=field_scratch, flops=int(1e7))
    state, scalar = dict(r=rhs), None
    for stage in range(ITERS):
        pieces, scalar = extend(parts, scalar)
        if stage == 2:
            scalar = reduce(scalar)
        new, scalar, parts = apply(stage, pieces, scalar, state)
        state.update(new)
    return call(
        final_kernel,
        (reduce(scalar), *(state[name] for name in "xrwpsz")),
        (f32(levels, columns),) * 2,
        scratch=(pltpu.VMEM((points // LANES, 16 * RATIO, LANES), jnp.float32),),
    )


def solution(mesh):
    in_specs = (
        P("lev", "patch"),
        P("lev", "patch"),
        P(None, "lev", "patch"),
        P("patch"),
        P("patch"),
        P(),
        P(),
    )
    out_specs = (P("lev", "patch"), P("lev", "patch"))
    return jax.shard_map(shards, mesh=mesh, in_specs=in_specs, out_specs=out_specs, check_vma=False)
```

```python
import functools

import jax
import jax.numpy as jnp
import numpy as np
from jax import lax
from jax.experimental import pallas as pl
from jax.experimental.pallas import tpu as pltpu
from jax.sharding import PartitionSpec as P

MEMBERS = 40
RATIO = 16
HALO = 128
ITERS = 4
LANES = 128
UNROLL = 8
REACH = 2 * HALO
VMEM_LIMIT = 24 * 1024 * 1024
GROUP = LANES * RATIO
PAIR = 2 * LANES


def tap_blocks():
    reach = np.arange(HALO + 1)
    rough = 0.5 + ((97 * reach * reach + 31 * reach) % 257) / 256.0
    raw = (1.0 - reach / (2.0 * HALO)) * rough
    taps = raw / np.sqrt(2.0 * np.sum(raw**2) - raw[0] ** 2)
    rows, cols = np.arange(HALO)[:, None], np.arange(HALO)[None, :]
    blocks = []
    for shift in range(3):
        distance = np.abs(rows - cols + (1 - shift) * HALO)
        blocks.append(np.where(distance <= HALO, taps[np.minimum(distance, HALO)], 0.0))
    return blocks


def block_products():
    blocks = tap_blocks()
    return np.stack([np.stack([a.T @ b for b in blocks]) for a in blocks]).astype(np.float32)


def band_kernel(levels, halo_ref, coupling_ref, prod_ref, hi_ref, lo_ref, coupling_out):
    first = lax.axis_index("lev") * levels - 1
    all_levels = coupling_ref.shape[0]
    coupling_out[...] = jnp.zeros_like(coupling_out)
    for k in range(levels + 2):
        at = jnp.clip(first + k, 0, all_levels - 1)
        value = jnp.where(at == first + k, coupling_ref[at], 0.0)
        coupling_out[pl.ds(k, 1), :] = jnp.full((1, LANES), value, jnp.float32)

    patch, patches = lax.axis_index("patch"), lax.axis_size("patch")
    counts = [halo_ref[lax.rem(patch + patches + step, patches)] for step in (-1, 0, 1)]
    own_blocks = hi_ref.shape[1] // HALO
    edge = (0, own_blocks + 1)
    lane = lax.broadcasted_iota(jnp.int32, (HALO, HALO), 1)
    row = lax.broadcasted_iota(jnp.int32, (HALO, HALO), 0)
    crossing = {
        (0, 2): (counts[0], False),
        (1, 1): (counts[1], True),
        (own_blocks, own_blocks + 2): (counts[1], False),
        (own_blocks + 1, own_blocks + 1): (counts[2], True),
    }

    def keep(index, key):
        count, from_end = crossing[key]
        return (HALO - 1 - index if from_end else index) < count

    for source in range(own_blocks + 4):
        for target in range(2, own_blocks + 2):
            total = jnp.zeros((HALO, HALO), jnp.float32)
            for i in range(edge[0], edge[1] + 1):
                a, b = source - i, target - i
                if not (0 <= a < 3 and 0 <= b < 3):
                    continue
                term = prod_ref[a, b]
                if (i, source) in crossing:
                    term = jnp.where(keep(row, (i, source)), term, 0.0)
                if (i, target) in crossing:
                    term = jnp.where(keep(lane, (i, target)), term, 0.0)
                total = total + term
            hi = total.astype(jnp.bfloat16)
            at = (pl.ds(source * HALO, HALO), pl.ds((target - 2) * HALO, HALO))
            hi_ref[at] = hi
            lo_ref[at] = (total - hi.astype(jnp.float32)).astype(jnp.bfloat16)


def to_subgrid(pert_ref, field_ref, weight_ref, part_refs, level_ref, side_ref):
    levels, ratio, points = field_ref.shape
    members = pert_ref.shape[1] // ratio
    tiles = members // 8

    def one_level(level):
        for lane_tile in range(points // LANES):
            lanes = pl.ds(lane_tile * LANES, LANES)
            field = field_ref[level, :, lanes]
            for j in range(3):
                level_ref[j] = field * weight_ref[j, lane_tile]
            def some_r(step, total, lanes=lanes):
                total = list(total)
                count = UNROLL * members
                at = pl.ds(pl.multiple_of(step * count, 8), count)
                perts = pert_ref.at[level, at, lanes]
                scales = level_ref.at[:, pl.ds(pl.multiple_of(step * UNROLL, UNROLL), UNROLL), :]
                for k in range(UNROLL):
                    scale = [scales[j, pl.ds(k, 8, stride=0), :] for j in range(3)]
                    for t in range(tiles):
                        pert = perts[k * members + 8 * t : k * members + 8 * t + 8, :]
                        for j in range(3):
                            total[j * tiles + t] += pert * scale[j]
                return tuple(total)

            zero = jnp.zeros((8, LANES), jnp.float32)
            total = lax.fori_loop(0, ratio // UNROLL, some_r, (zero,) * (3 * tiles))
            total = [total[j * tiles : (j + 1) * tiles] for j in range(3)]
            for j in range(3):
                for t in range(tiles):
                    side_ref[j, pl.ds(8 * t, 8), lanes] = total[j][t]
        return (
            side_ref[1]
            + pltpu.roll(side_ref[0], points - 1, axis=1)
            + pltpu.roll(side_ref[2], 1, axis=1)
        )

    odd = lax.rem(lax.axis_index("lev"), 2)
    firsts = ((1 - odd) * (levels - 2), 2, odd * (levels - 2))
    for first, ref in zip(firsts, part_refs):
        count = ref.shape[0] // members

        def body(k, carry, ref=ref, first=first):
            rows = pl.ds(pl.multiple_of(k * members, 8), members)
            ref[rows, :] = one_level(first + k)
            return carry

        lax.fori_loop(0, count, body, 0)


def from_subgrid(pert_ref, level, values, weight_ref, side_ref, sum_ref, out_ref):
    members, points = values.shape
    ratio = out_ref.shape[0]
    tiles = members // 8
    side_ref[0] = pltpu.roll(values, 1, axis=1)
    side_ref[1] = values
    side_ref[2] = pltpu.roll(values, points - 1, axis=1)
    for lane_tile in range(points // LANES):
        lanes = pl.ds(lane_tile * LANES, LANES)
        near = [[side_ref[j, pl.ds(8 * t, 8), lanes] for t in range(tiles)] for j in range(3)]
        def some_r(step, carry, lanes=lanes, near=near, lane_tile=lane_tile):
            count = UNROLL * members
            at = pl.ds(pl.multiple_of(step * count, 8), count)
            perts = pert_ref.at[level, at, lanes]
            some = pl.ds(pl.multiple_of(step * UNROLL, UNROLL), UNROLL)
            weights = weight_ref.at[:, lane_tile, some, :]
            count = 8 * UNROLL
            sum_at = sum_ref.at[pl.ds(pl.multiple_of(step * count, 8), count), :]
            for k in range(UNROLL):
                total = [None] * 3
                for t in range(tiles):
                    pert = perts[k * members + 8 * t : k * members + 8 * t + 8, :]
                    for j in range(3):
                        term = pert * near[j][t]
                        total[j] = term if total[j] is None else total[j] + term
                mixed = None
                for j in range(3):
                    term = total[j] * weights[j, pl.ds(k, 8, stride=0), :]
                    mixed = term if mixed is None else mixed + term
                sum_at[8 * k : 8 * k + 8, :] = mixed
            return carry

        lax.fori_loop(0, ratio // UNROLL, some_r, 0)
        result = sum_ref[pl.ds(0, ratio, stride=8), :]
        for k in range(1, 8):
            result = result + sum_ref[pl.ds(k, ratio, stride=8), :]
        out_ref[:, lanes] = result


def split(x):
    hi = x.astype(jnp.bfloat16)
    return hi, (x - hi.astype(jnp.float32)).astype(jnp.bfloat16)


def band_product(pieces, hi_ref, lo_ref, out_ref):
    even = lax.rem(lax.axis_index("patch"), 2) == 0
    halves = [split(jnp.where(even, a[...], b[...])) for a, b in zip(pieces, pieces[::-1])]
    for block in range(out_ref.shape[1] // REACH):
        cols = pl.ds(block * REACH, REACH)
        total = None
        for k in range(block, block + 3):
            hi, lo = halves[k]
            rows = pl.ds(k * REACH, REACH)
            for left, right_ref in ((hi, hi_ref), (lo, hi_ref), (hi, lo_ref)):
                term = jnp.dot(left, right_ref[rows, cols], preferred_element_type=jnp.float32)
                total = term if total is None else total + term
        out_ref[:, cols] = total


def wide(x, points):
    return jnp.concatenate([x] * (points // LANES), axis=1)


def totals(dots_ref, count):
    total = jnp.sum(dots_ref[...], axis=0)
    lane = lax.broadcasted_iota(jnp.int32, total.shape, 1)
    picked = [jnp.sum(jnp.where(lane == k, total, 0.0), keepdims=True) for k in range(count)]
    return [jnp.broadcast_to(x, total.shape) for x in picked]


def first_pair(dots_ref):
    rr, rw, ww, wn, nn = totals(dots_ref, 5)
    alpha0 = rr / rw
    gamma1 = rr - 2.0 * alpha0 * rw + alpha0 * alpha0 * ww
    beta1 = gamma1 / rr
    r1_w = rw - alpha0 * ww
    r1_w1 = rw - 2.0 * alpha0 * ww + alpha0 * alpha0 * wn
    w1_w = ww - alpha0 * wn
    w1_w1 = ww - 2.0 * alpha0 * wn + alpha0 * alpha0 * nn
    p1_s1 = r1_w1 + 2.0 * beta1 * r1_w + beta1 * beta1 * rw
    alpha1 = gamma1 / p1_s1
    r1_s1 = r1_w1 + beta1 * r1_w
    s1_s1 = w1_w1 + 2.0 * beta1 * w1_w + beta1 * beta1 * ww
    gamma2 = gamma1 - 2.0 * alpha1 * r1_s1 + alpha1 * alpha1 * s1_s1
    return alpha0, beta1, alpha1, gamma2 / gamma1


def last_pair(dots_ref):
    rr, rw, rs, ss, ws, zs, ps = totals(dots_ref, 7)
    alpha = rr / ps
    gamma = rr - 2.0 * alpha * rs + alpha * alpha * ss
    beta = gamma / rr
    r_w = rw - 2.0 * alpha * ws + alpha * alpha * zs
    p_s = r_w + 2.0 * beta * (rs - alpha * ss) + beta * beta * ps
    return alpha, beta, gamma / p_s


STATE_IN = {0: "r", 1: "rw", 2: "rwn", 3: "rwpsz"}
STATE_OUT = {0: "w", 1: "n", 2: "xrwpsz", 3: "z"}
NEXT = {0: "w", 1: "n", 2: "w"}


def apply_kernel(stage, parts, *refs):
    refs = list(refs)
    take = lambda n: [refs.pop(0) for _ in range(n)]
    pieces = take(4)
    hi_ref, lo_ref, pert_ref, weight_ref, error_ref = take(5)
    (scalar_in,) = take(1) if stage >= 2 else (None,)
    state = dict(zip(STATE_IN[stage], take(len(STATE_IN[stage]))))
    new = dict(zip(STATE_OUT[stage], take(len(STATE_OUT[stage]))))
    (scalar_out,) = take(1) if stage else (None,)
    part_refs = take(parts)
    conv_ref, side_ref, level_ref, sum_ref, image_ref = refs

    levels, ratio, points = error_ref.shape
    members = pert_ref.shape[1] // ratio
    band_product(pieces, hi_ref, lo_ref, conv_ref)

    if stage == 2:
        steps = first_pair(scalar_in)
        scalar_out[0:1] = steps[3]
        alpha0, beta1, alpha1, beta2 = [wide(x, points) for x in steps]
    if stage == 3:
        beta2 = wide(scalar_in[0:1], points)
    counts = {0: 0, 1: 5, 2: 0, 3: 7}[stage]

    def one_level(level, carry):
        rows = pl.ds(pl.multiple_of(level * members, 8), members)
        from_subgrid(pert_ref, level, conv_ref[rows, :], weight_ref, side_ref, sum_ref, image_ref)
        mean = image_ref[...] * (1.0 / (MEMBERS - 1))
        old = {name: ref[level] for name, ref in state.items()}
        if stage == 0:
            new["w"][level] = error_ref[level] * old["r"] + mean
            products = []
        elif stage == 1:
            r, w = old["r"], old["w"]
            n = error_ref[level] * w + mean
            new["n"][level] = n
            products = [r * r, r * w, w * w, w * n, n * n]
        elif stage == 2:
            r, w, n = old["r"], old["w"], old["n"]
            m = error_ref[level] * n + mean
            r1, w1, n1 = r - alpha0 * w, w - alpha0 * n, n - alpha0 * m
            p, s, z = r1 + beta1 * r, w1 + beta1 * w, n1 + beta1 * n
            new["x"][level] = alpha0 * r + alpha1 * p
            r, w = r1 - alpha1 * s, w1 - alpha1 * z
            new["r"][level] = r
            new["w"][level] = w
            new["p"][level] = r + beta2 * p
            new["s"][level] = w + beta2 * s
            new["z"][level] = z
            products = []
        else:
            r, w, p, s = (old[name] for name in "rwps")
            z = error_ref[level] * w + mean + beta2 * old["z"]
            new["z"][level] = z
            products = [r * r, r * w, r * s, s * s, w * s, z * s, p * s]
        return tuple(c + sum(x[k : k + 8] for k in range(0, ratio, 8)) for c, x in zip(carry, products))

    zero = jnp.zeros((8, points), jnp.float32)
    total = lax.fori_loop(0, levels, one_level, (zero,) * counts)
    if counts:
        lane = lax.broadcasted_iota(jnp.int32, (1, LANES), 1)
        row = jnp.zeros((1, LANES), jnp.float32)
        for k, t in enumerate(total):
            row = jnp.where(lane == k, jnp.sum(t, keepdims=True), row)
        scalar_out[...] = jnp.broadcast_to(row[None], scalar_out.shape)
    if parts:
        to_subgrid(pert_ref, new[NEXT[stage]], weight_ref, part_refs, level_ref, side_ref)


def final_kernel(dots_ref, x_ref, r_ref, w_ref, p_ref, s_ref, z_ref, x_out, r_out, stack_ref):
    levels, ratio, points = x_ref.shape
    alpha2, beta3, alpha3 = last_pair(dots_ref)
    matrices = permutations(transposed=True)
    rows = stack_ref.shape[1] // ratio
    stack_ref[...] = jnp.zeros_like(stack_ref)
    groups = []
    for group in range(points // LANES):
        lanes = pl.ds(group * LANES, LANES)
        for level in range(levels):
            r, w, p, s = (ref[level, :, lanes] for ref in (r_ref, w_ref, p_ref, s_ref))
            r3 = r - alpha2 * s
            w3 = w - alpha2 * z_ref[level, :, lanes]
            x = x_ref[level, :, lanes] + alpha2 * p + alpha3 * (r3 + beta3 * p)
            stack_ref[group, pl.ds(level * ratio, ratio), :] = x
            r4 = r3 - alpha3 * (w3 + beta3 * s)
            stack_ref[group, pl.ds((8 + level) * ratio, ratio), :] = r4
        groups.append(
            [two_terms(stack_ref[group, pl.ds(r, rows, stride=ratio), :]) for r in range(ratio)]
        )
    for group, tiles in enumerate(turn_back(groups, matrices)):
        for t, tile in enumerate(tiles):
            tile = sum_of_terms(tile)
            cols = pl.ds(group * GROUP + t * LANES, LANES)
            x_out[:, cols] = tile[:levels]
            r_out[:, cols] = tile[8 : 8 + levels]


def vertical_kernel(
    coupling_ref, far_recv, far_own, middle, near_own, near_recv, far_ref, near_ref
):
    lev_odd = lax.rem(lax.axis_index("lev"), 2)
    patch_odd = lax.rem(lax.axis_index("patch"), 2)
    points = middle.shape[1]
    blocks = (far_recv, far_own, middle, near_own, near_recv)
    levels = sum(ref.shape[0] for ref in blocks) // MEMBERS - 4

    def run(blocks, left_ref, right_ref):
        where = [(ref, k * MEMBERS) for ref in blocks for k in range(ref.shape[0] // MEMBERS)]
        coupling = [wide(coupling_ref[pl.ds(k, 8, stride=0), :], points) for k in range(levels + 2)]

        def body(t, carry):
            row = pl.multiple_of(t * 8, 8)
            field = [ref[pl.ds(base + row, 8), :] for ref, base in where]
            stepped = [
                field[l + 1] + coupling[l] * (field[l] + field[l + 2]) for l in range(levels + 2)
            ]
            scaled = [coupling[l] * stepped[l] for l in range(levels + 2)]
            for l in range(levels):
                value = stepped[l + 1] + (scaled[l] + scaled[l + 2])
                rows = pl.ds(l * MEMBERS + row, 8)
                left_ref[rows, :] = value[:, :REACH]
                right_ref[rows, :] = value[:, points - REACH :]
            return carry

        lax.fori_loop(0, MEMBERS // 8, body, 0)

    for lev_is_odd in range(2):
        for patch_is_odd in range(2):
            order = blocks[::-1] if lev_is_odd else blocks
            sides = (near_ref, far_ref) if patch_is_odd else (far_ref, near_ref)

            @pl.when((lev_odd == lev_is_odd) & (patch_odd == patch_is_odd))
            def _(order=order, sides=sides):
                run(order, *sides)


def permutations(transposed=False):
    row = lax.broadcasted_iota(jnp.int32, (PAIR, PAIR), 1 if transposed else 0)
    col = lax.broadcasted_iota(jnp.int32, (PAIR, PAIR), 0 if transposed else 1)
    targets = [(row % 16) * 16 + row // 16]
    for kept in (2, 1, 0):
        low = 6 - kept
        new, out = row // 128, (row // 64) % 2
        middle, rest = (row % 64) >> low, row % (1 << low)
        targets.append(out * 128 + (middle << (low + 1)) + (new << low) + rest)
    return [jnp.where(target == col, 1.0, 0.0).astype(jnp.bfloat16) for target in targets]


def reorder(tiles):
    return [tiles[sum(((r >> i) & 1) << (3 - i) for i in range(4))] for r in range(16)]


def permute_pairs(groups, bit, matrix):
    rows = groups[0][0].shape[0]
    pairs = [(g, k, k + bit) for g in range(len(groups)) for k in range(16) if not k & bit]
    stacked = [jnp.concatenate([groups[g][a], groups[g][b]], axis=1) for g, a, b in pairs]
    stacked = jnp.concatenate(stacked, axis=0).astype(jnp.bfloat16)
    turned = jnp.dot(stacked, matrix, preferred_element_type=jnp.float32)
    result = [[None] * 16 for _ in groups]
    for i, (g, *pair) in enumerate(pairs):
        for half, k in enumerate(pair):
            lanes = slice(half * LANES, (half + 1) * LANES)
            result[g][k] = turned[i * rows : (i + 1) * rows, lanes]
    return result


def turn(groups, matrices):
    for bit, matrix in zip((1, 2, 4, 8), matrices):
        groups = permute_pairs(groups, bit, matrix)
    return [reorder(tiles) for tiles in groups]


def turn_back(groups, matrices):
    groups = [reorder(tiles) for tiles in groups]
    for bit, matrix in reversed(list(zip((1, 2, 4, 8), matrices))):
        groups = permute_pairs(groups, bit, matrix)
    return groups


def two_terms(x):
    hi = x.astype(jnp.bfloat16).astype(jnp.float32)
    return jnp.concatenate([hi, x - hi], axis=0)


def sum_of_terms(x):
    rows = x.shape[0] // 2
    return x[:rows] + x[rows:]


def turn_fields(stack_ref, turn_ref, matrices, take):
    rows, columns = stack_ref.shape
    groups = [
        [two_terms(stack_ref[:, pl.ds(g * GROUP + t * LANES, LANES)]) for t in range(RATIO)]
        for g in range(columns // GROUP)
    ]
    for group, tiles in enumerate(turn(groups, matrices)):
        for r, tile in enumerate(tiles):
            turn_ref[group, pl.ds(r * rows, rows), :] = sum_of_terms(tile)
        take(group, lambda f: turn_ref[group, pl.ds(f, RATIO, stride=rows), :])


def error_kernel(error_ref, error_out, stack_ref, turn_ref):
    levels = error_ref.shape[0]
    stack_ref[...] = jnp.zeros_like(stack_ref)
    stack_ref[0:levels] = error_ref[...]

    def take(group, picked):
        for level in range(levels):
            error_out[level, :, pl.ds(group * LANES, LANES)] = picked(level)

    turn_fields(stack_ref, turn_ref, permutations(), take)


def start_kernel(
    parts,
    rhs_ref,
    slot_ref,
    weight_ref,
    pert_ref,
    field_ref,
    weight_out,
    pert_out,
    *refs,
):
    part_refs = refs[:parts]
    stack_ref, turn_ref, level_ref, side_ref = refs[parts:]
    levels, members, columns = pert_ref.shape

    stack_ref[0:levels] = rhs_ref[...]
    weight = weight_ref[...]
    column = lax.broadcasted_iota(jnp.int32, weight.shape, 1)
    is_lower = slot_ref[...] < column // RATIO
    stack_ref[levels : levels + 1] = jnp.where(is_lower, weight, 0.0)
    stack_ref[levels + 1 : levels + 2] = jnp.where(is_lower, 1.0 - weight, weight)
    stack_ref[levels + 2 : levels + 3] = jnp.where(is_lower, 0.0, 1.0 - weight)
    matrices = permutations()

    def take(group, picked):
        for level in range(levels):
            field_ref[level, :, pl.ds(group * LANES, LANES)] = picked(level)
        for j in range(3):
            weight_out[j, group] = picked(levels + j)

    turn_fields(stack_ref, turn_ref, matrices, take)

    for level in range(levels):
        groups = [
            [
                pert_ref[level, :, pl.ds(g * GROUP + t * LANES, LANES)].astype(jnp.float32)
                for t in range(16)
            ]
            for g in range(columns // GROUP)
        ]
        for group, tiles in enumerate(turn(groups, matrices)):
            for r, tile in enumerate(tiles):
                at = pl.ds(r * members, members)
                pert_out[level, at, pl.ds(group * LANES, LANES)] = tile
    to_subgrid(pert_out, field_ref, weight_out, part_refs, level_ref, side_ref)


def whole():
    return pl.BlockSpec(memory_space=pltpu.VMEM)


def scalars():
    return pl.BlockSpec(memory_space=pltpu.SMEM)


def call(kernel, args, out_shape, scratch=(), flops=0, in_specs=None):
    size = sum(np.prod(a.shape) * a.dtype.itemsize for a in args)
    return pl.pallas_call(
        kernel,
        in_specs=in_specs or [whole()] * len(args),
        out_specs=jax.tree.map(lambda _: whole(), out_shape),
        out_shape=out_shape,
        scratch_shapes=list(scratch),
        compiler_params=pltpu.CompilerParams(vmem_limit_bytes=VMEM_LIMIT),
        cost_estimate=pl.CostEstimate(flops=flops, bytes_accessed=int(size), transcendentals=0),
    )(*args)


def f32(*shape):
    return jax.ShapeDtypeStruct(shape, jnp.float32)


def swap(block, axis, first, periodic):
    count = lax.axis_size(axis)
    pairs = []
    for a in range(first, count, 2):
        b = (a + 1) % count
        if periodic or b > a:
            pairs += [(a, b), (b, a)]
    return lax.ppermute(block, axis, pairs)


def shards(
    increment_rhs,
    error_variance,
    perturbations,
    interp_slot,
    interp_weight,
    halo_rows,
    vertical_coupling,
):
    members, levels, columns = perturbations.shape
    points = columns // RATIO
    devices = lax.axis_size("patch") * lax.axis_size("lev")

    extended = points + 2 * REACH
    band_hi, band_lo, couplings = call(
        functools.partial(band_kernel, levels),
        (halo_rows, vertical_coupling, jnp.asarray(block_products())),
        (
            jax.ShapeDtypeStruct((extended, points), jnp.bfloat16),
            jax.ShapeDtypeStruct((extended, points), jnp.bfloat16),
            f32(8 * pl.cdiv(levels + 2, 8), LANES),
        ),
        in_specs=[scalars(), scalars(), whole()],
    )
    part_levels = (2, levels - 4, 2)
    part_shapes = tuple(f32(n * members, points) for n in part_levels)
    level_scratch = pltpu.VMEM((3, RATIO, LANES), jnp.float32)
    side_scratch = pltpu.VMEM((3, members, points), jnp.float32)
    grid_shape = f32(levels, RATIO, points)

    def extend(parts, dots):
        near, middle, far = parts
        far_recv = swap(far, "lev", 1, False)
        near_recv = swap(near, "lev", 0, False)
        half = f32(levels * members, REACH)
        far, near = call(
            vertical_kernel,
            (couplings, far_recv, far, middle, near, near_recv),
            (half, half),
        )
        if dots is not None:
            dots, far, near = lax.optimization_barrier((dots, far, near))
        far_recv = swap(far, "patch", 1, True)
        near_recv = swap(near, "patch", 0, True)
        return (far_recv, far, near, near_recv), dots

    def reduce(dots):
        return lax.all_to_all(dots, ("patch", "lev"), 0, 0, tiled=True)

    def apply(stage, pieces, scalar, state):
        last = stage == ITERS - 1
        outs = [grid_shape] * len(STATE_OUT[stage])
        outs += {0: [], 2: [f32(8, LANES)]}.get(stage, [f32(devices, 1, LANES)])
        outs += [] if last else list(part_shapes)
        args = [*pieces, band_hi, band_lo, pert, weights, error]
        args += [scalar] if stage >= 2 else []
        args += [state[name] for name in STATE_IN[stage]]
        result = list(
            call(
                functools.partial(apply_kernel, stage, 0 if last else 3),
                args,
                tuple(outs),
                scratch=(
                    pltpu.VMEM((levels * members, points), jnp.float32),
                    side_scratch,
                    level_scratch,
                    pltpu.VMEM((8 * RATIO, LANES), jnp.float32),
                    pltpu.VMEM((RATIO, points), jnp.float32),
                ),
                flops=int(1e9),
            )
        )
        new = {name: result.pop(0) for name in STATE_OUT[stage]}
        return new, result.pop(0) if stage else None, result

    field_rows = 8 * pl.cdiv(levels + 3, 8)
    field_scratch = (
        pltpu.VMEM((field_rows, columns), jnp.float32),
        pltpu.VMEM((points // LANES, field_rows * RATIO, LANES), jnp.float32),
    )
    rhs, weights, pert, *parts = call(
        functools.partial(start_kernel, 3),
        (
            increment_rhs,
            interp_slot[None],
            interp_weight[None],
            perturbations.transpose(1, 0, 2),
        ),
        (
            grid_shape,
            f32(3, points // LANES, RATIO, LANES),
            f32(levels, RATIO * members, points),
            *part_shapes,
        ),
        scratch=(
            *field_scratch,
            level_scratch,
            side_scratch,
        ),
        flops=int(1e8),
    )
    error = call(error_kernel, (error_variance,), grid_shape, scratch=field_scratch, flops=int(1e7))
    state, scalar = dict(r=rhs), None
    for stage in range(ITERS):
        pieces, scalar = extend(parts, scalar)
        if stage == 2:
            scalar = reduce(scalar)
        new, scalar, parts = apply(stage, pieces, scalar, state)
        state.update(new)
    return call(
        final_kernel,
        (reduce(scalar), *(state[name] for name in "xrwpsz")),
        (f32(levels, columns),) * 2,
        scratch=(pltpu.VMEM((points // LANES, 16 * RATIO, LANES), jnp.float32),),
    )


def solution(mesh):
    in_specs = (
        P("lev", "patch"),
        P("lev", "patch"),
        P(None, "lev", "patch"),
        P("patch"),
        P("patch"),
        P(),
        P(),
    )
    out_specs = (P("lev", "patch"), P("lev", "patch"))
    return jax.shard_map(shards, mesh=mesh, in_specs=in_specs, out_specs=out_specs, check_vma=False)
```
